256 devices in a mesh: seq: 32 (over y, z_lo, core), head: 8 (over x, z_hi).
Axes of the slice: x: 4, y: 4, z: 8 (z_hi: 2, z_lo: 4; z = z_hi * 4 + z_lo), core: 2. Of those that a mesh axis runs over, the one named last changes fastest.
Arguments:
- queries: bfloat16 [4096, 16384], P('seq', 'head'), may hold values from -16 to 16
- keys: bfloat16 [4096, 1024], P('seq', 'head'), may hold values from -12 to 12
- values: bfloat16 [4096, 1024], P('seq', 'head'), may hold values from -6 to 6
- feat_q: bfloat16 [128, 128, 128], P('head'), may hold values from -0.6 to 0.6
- feat_k: bfloat16 [128, 128, 128], P('head'), may hold values from -0.6 to 0.6
Outputs:
- student: bfloat16 [4096, 16384], P('seq', 'head')
- token_loss: float32 [4096], P(('seq', 'head'))
The draws below stay inside these ranges and needn't reach their ends.
All inputs are finite; a program needn't handle non-finite values.
Results may differ from the reference program's by a relative error of at most 0.0035.
Values may be sent and summed in bfloat16 or wider, within the bound.
No kernel may reach another device: no remote copies, remote signals or barrier semaphores. Data moves between devices by JAX's collectives and lax.ppermute only.
A program may use at most 128 MiB of HBM per device.

```python
import math
import jax
import jax.numpy as jnp
from jax import lax

HD = 128
HQ = 128
KVH = 8
GROUP = 16
TOKENS = 4096


def draw_queries(key, part):
    base = jax.random.truncated_normal(jax.random.fold_in(key, 1), -6.0, 6.0, (TOKENS, HQ * HD), jnp.float32)
    return base.astype(jnp.bfloat16)


def draw_keys(key, part):
    base = jax.random.truncated_normal(jax.random.fold_in(key, 2), -6.0, 6.0, (TOKENS, KVH * HD), jnp.float32)
    return base.astype(jnp.bfloat16)


def feature_weights(key, salt):
    limit = 1.0 / math.sqrt(HD)
    base = jax.random.truncated_normal(jax.random.fold_in(key, salt), -3.0, 3.0, (HQ, HD, HD), jnp.float32) * limit
    return base


def draw_feat_q(key, part):
    return feature_weights(key, 3).astype(jnp.bfloat16)


def draw_feat_k(key, part):
    return feature_weights(key, 4).astype(jnp.bfloat16)


def steps_of(key, shape, shards, low, high):
    def one(axis_at, parts):
        heights = jax.random.uniform(jax.random.fold_in(jax.random.fold_in(key, 6), axis_at), (parts,), jnp.float32, low / len(shards), high / len(shards))
        return jnp.repeat(jnp.exp(heights), shape[axis_at] // parts).reshape((-1,) + (1,) * (len(shape) - axis_at - 1))

    gain = one(*shards[0])
    for cut in shards[1:]:
        gain = gain * one(*cut)
    return gain


def scatter_about(rng, extent, spread, most, pieces=(), held_as=jnp.bfloat16):
    values = spread * jax.random.normal(rng, extent, jnp.float32)
    if pieces:
        values = values * steps_of(rng, extent, pieces, -0.22, 0.18)
    return jnp.clip(values, -most, most).astype(held_as)


def setup_inputs(seed: int = 0) -> dict:
    arg_keys = jax.random.split(jax.random.key(seed), 6)
    return {
        "queries": draw_queries(jax.random.fold_in(arg_keys[5], 71), 0),
        "keys": draw_keys(jax.random.fold_in(arg_keys[5], 71), 0),
        "values": scatter_about(arg_keys[2], (TOKENS, KVH * HD), 1.0, 6.0, ((0, 32), (1, 8))),
        "feat_q": draw_feat_q(jax.random.fold_in(arg_keys[5], 71), 0),
        "feat_k": draw_feat_k(jax.random.fold_in(arg_keys[5], 71), 0),
    }


exact_mode = lax.Precision.HIGHEST

def feature(inputs, weights):
    logits = jnp.einsum('htd,hde->hte', inputs.astype(jnp.float32), weights.astype(jnp.float32), precision=exact_mode)
    return jnp.concatenate([jax.nn.softmax(logits, -1), jax.nn.softmax(-logits, -1)], -1).astype(jnp.bfloat16)

def one_group(operands):
    query_heads, key_head, value_head, weight_query, weight_key = operands
    per_group = query_heads.shape[0]
    length = key_head.shape[0]
    head_dim = key_head.shape[1]
    score_scale = 1.0 / math.sqrt(head_dim)
    key_float = key_head.astype(jnp.float32)
    value_float = value_head.astype(jnp.float32)
    block_rows = math.gcd(length, 512)
    key_position = jnp.arange(length, dtype=jnp.int32)

    def teach_block(block_index):
        first_row = (block_index * block_rows).astype(jnp.int32)
        query_block = lax.dynamic_slice_in_dim(query_heads, first_row, block_rows, 1).astype(jnp.float32)
        scores = jnp.einsum('rqd,kd->rqk', query_block, key_float, precision=exact_mode) * score_scale
        query_position = first_row + jnp.arange(block_rows, dtype=jnp.int32)
        allowed = key_position[None, :] <= query_position[:, None]
        scores = jnp.where(allowed[None], scores, -jnp.inf)
        row_max = scores.max(-1, keepdims=True)
        exponent = jnp.exp(scores - row_max)
        weight_sum = exponent.sum(-1)
        weights = exponent.astype(jnp.bfloat16)
        mixed = jnp.einsum('rqk,kd->rqd', weights.astype(jnp.float32), value_float, precision=exact_mode)
        return mixed / weight_sum[..., None]
    teacher = lax.map(teach_block, jnp.arange(length // block_rows, dtype=jnp.int32))
    teacher = teacher.transpose(1, 0, 2, 3).reshape(per_group, length, head_dim)
    query_feats = feature(query_heads, weight_query).astype(jnp.float32)
    key_feats = feature(jnp.broadcast_to(key_head, (per_group,) + key_head.shape), weight_key).astype(jnp.float32)
    feat_count = query_feats.shape[2]
    student_rows = math.gcd(length, 512)
    block_count = length // student_rows
    query_blocks = query_feats.reshape(per_group, block_count, student_rows, feat_count).transpose(1, 0, 2, 3)
    key_blocks = key_feats.reshape(per_group, block_count, student_rows, feat_count).transpose(1, 0, 2, 3)
    value_blocks = value_float.reshape(block_count, student_rows, head_dim)
    lower_mask = jnp.tril(jnp.ones((student_rows, student_rows), jnp.float32))

    def advance(running, operand):
        state, key_sum = running
        query_part, key_part, value_part = operand
        local_scores = jnp.einsum('rqf,rkf->rqk', query_part, key_part, precision=exact_mode) * lower_mask
        numerator = jnp.einsum('rqk,kd->rqd', local_scores, value_part, precision=exact_mode)
        numerator = numerator + jnp.einsum('rqf,rfd->rqd', query_part, state, precision=exact_mode)
        denominator = local_scores.sum(-1) + jnp.einsum('rqf,rf->rq', query_part, key_sum, precision=exact_mode)
        state = state + jnp.einsum('rkf,kd->rfd', key_part, value_part, precision=exact_mode)
        key_sum = key_sum + key_part.sum(1)
        return ((state, key_sum), numerator / denominator[..., None])
    start_state = (jnp.zeros((per_group, feat_count, head_dim), jnp.float32), jnp.zeros((per_group, feat_count), jnp.float32))
    _, student = lax.scan(advance, start_state, (query_blocks, key_blocks, value_blocks))
    student = student.transpose(1, 0, 2, 3).reshape(per_group, length, head_dim)
    loss_terms = ((student - teacher) ** 2).sum((0, 2)) / HQ
    return (student, loss_terms)

def reference(queries, keys, values, feat_q, feat_k):
    length = queries.shape[0]
    query_heads = queries.reshape(length, KVH, GROUP, HD).transpose(1, 2, 0, 3)
    key_heads = keys.reshape(length, KVH, HD).transpose(1, 0, 2)
    value_heads = values.reshape(length, KVH, HD).transpose(1, 0, 2)
    weight_query = feat_q.reshape(KVH, GROUP, HD, HD)
    weight_key = feat_k.reshape(KVH, GROUP, HD, HD)
    student, loss_terms = lax.map(one_group, (query_heads, key_heads, value_heads, weight_query, weight_key))
    student_out = student.transpose(2, 0, 1, 3).reshape(length, HQ * HD).astype(jnp.bfloat16)
    return (student_out, loss_terms.sum(0))
```

```python
import math

import jax
import jax.numpy as jnp
from jax import lax
from jax.experimental import pallas as pl
from jax.experimental.pallas import tpu as pltpu
from jax.sharding import Mesh
from jax.sharding import PartitionSpec as P

HQ = 128
D = 128
F = 2 * D
LOG2E = math.log2(math.e)
SCALE = LOG2E / math.sqrt(D)
NEG = -1e30
SEQ = ("y", "z", "c")
F32, BF16 = jnp.float32, jnp.bfloat16
VMEM = pl.BlockSpec(memory_space=pltpu.VMEM)
SMEM = pl.BlockSpec(memory_space=pltpu.SMEM)


def mm(a, b):
    return jnp.dot(a, b, preferred_element_type=F32)


def mm_t(a, b):
    return lax.dot_general(a, b, (((1,), (1,)), ((), ())), preferred_element_type=F32)


def split(x):
    high = x.astype(BF16)
    return high, (x - high.astype(F32)).astype(BF16)


def both_softmax(x, axis):
    up = jnp.exp2(x - jnp.max(x, axis, keepdims=True))
    down = jnp.exp2(jnp.min(x, axis, keepdims=True) - x)
    up = up * (1.0 / jnp.sum(up, axis, keepdims=True))
    down = down * (1.0 / jnp.sum(down, axis, keepdims=True))
    return up.astype(BF16), down.astype(BF16)


def scaled_queries(q_ref, h):
    q = q_ref[:, pl.ds(pl.multiple_of(h * D, D), D)].astype(F32) * SCALE
    return jnp.concatenate(split(q), 1)


def key_features(w2, k2):
    return jnp.concatenate(both_softmax(mm_t(w2, k2), 0), 0)


def one_column(rows):
    return (lax.broadcasted_iota(jnp.int32, (rows, D), 1) == 0).astype(F32).astype(BF16)


def fill(k2_ref, v1_ref, at, kv):
    rows = kv.shape[0]
    k2_ref[at : at + rows, :D] = kv[:, :D]
    k2_ref[at : at + rows, D:] = kv[:, :D]
    v1_ref[at : at + rows, :D] = kv[:, D:]
    v1_ref[at : at + rows, D:] = one_column(rows)


def prepare(q_ref, fq_ref, fk_ref, qf_ref, wk_ref):
    def head(h, _):
        q = q_ref[:, pl.ds(pl.multiple_of(h * D, D), D)]
        up, down = both_softmax(mm(q, fq_ref[h]) * LOG2E, 1)
        qf_ref[h, :, :D] = up
        qf_ref[h, :, D:] = down
        high, low = split((fk_ref[h].astype(F32) * LOG2E).T)
        wk_ref[h, :, :D] = high
        wk_ref[h, :, D:] = low
        return 0

    lax.fori_loop(0, fq_ref.shape[0], head, 0, unroll=2)


def own_row(at_ref, q_ref, qf_ref, wk_ref, mine_ref, other_ref, acc_ref, m_ref, near_ref, k2, v1, bias, keep):
    tokens = q_ref.shape[0]
    half = mine_ref.shape[0]
    z, c = at_ref[1], at_ref[2]
    fill(k2, v1, 0, mine_ref[...])
    fill(k2, v1, half, other_ref[...])
    row = lax.broadcasted_iota(jnp.int32, (tokens, tokens), 0)
    col = lax.broadcasted_iota(jnp.int32, (tokens, tokens), 1)
    for slot in range(half // tokens):
        for side in range(2):
            if slot == 0 and side == 0:
                seen = (col <= row).astype(F32)
            else:
                allowed = slot <= z if slot else c == 1
                seen = jnp.full((tokens, tokens), jnp.where(allowed, 1.0, 0.0), F32)
            at = side * half + slot * tokens
            keep[:, at : at + tokens] = seen
            bias[:, at : at + tokens] = (1.0 - seen) * NEG

    def head(h, _):
        s = mm_t(scaled_queries(q_ref, h), k2[...]) + bias[...]
        m = jnp.max(s, 1, keepdims=True)
        p = jnp.exp2(s - m).astype(BF16)
        acc_ref[h] = mm(p, v1[...])
        m_ref[h] = jnp.broadcast_to(m, (tokens, D))
        kf = key_features(wk_ref[h], k2[...])
        a = (mm(qf_ref[h], kf) * keep[...]).astype(BF16)
        near_ref[h] = mm(a, v1[...])
        return 0

    lax.fori_loop(0, qf_ref.shape[0], head, 0)


def earlier_state(at_ref, wk_ref, *refs):
    rows, (out_ref, k2, v1, state, sums) = refs[:-5], refs[-5:]
    heads = wk_ref.shape[0]
    state[...] = jnp.zeros_like(state)
    for k, row_ref in enumerate(rows):

        @pl.when(at_ref[0] > k)
        def _(row_ref=row_ref):
            fill(k2, v1, 0, row_ref[...])

            def head(h, _):
                state[h] += mm(key_features(wk_ref[h], k2[...]), v1[...])
                return 0

            lax.fori_loop(0, heads, head, 0)

    lane = lax.broadcasted_iota(jnp.int32, (F, D), 1)
    sums[...] = jnp.zeros_like(sums)
    for h in range(heads):
        out_ref[h] = state[h, :, :D].astype(BF16)
        high, low = split(state[h, :, D : D + 1])
        sums[...] += jnp.where(lane == h, high.astype(F32), 0.0) + jnp.where(
            lane == heads + h, low.astype(F32), 0.0
        )
    out_ref[heads] = sums[...].astype(BF16)


def earlier_teacher(at_ref, q_ref, acc0_ref, m0_ref, *refs):
    rows, (out_ref, k2, v1, acc, m_all) = refs[:-5], refs[-5:]
    heads = acc0_ref.shape[0]
    half = rows[0].shape[0]
    acc[...] = acc0_ref[...]
    m_all[...] = m0_ref[...]
    for k in range(len(rows) // 2):

        @pl.when(at_ref[0] > k)
        def _(k=k):
            fill(k2, v1, 0, rows[2 * k][...])
            fill(k2, v1, half, rows[2 * k + 1][...])

            def head(h, _):
                s = mm_t(scaled_queries(q_ref, h), k2[...])
                before = m_all[h][:, :1]
                m = jnp.maximum(before, jnp.max(s, 1, keepdims=True))
                p = jnp.exp2(s - m).astype(BF16)
                acc[h] = acc[h] * jnp.exp2(before - m) + mm(p, v1[...])
                m_all[h] = jnp.broadcast_to(m, m_all.shape[1:])
                return 0

            lax.fori_loop(0, heads, head, 0)

    def finish(h, _):
        out_ref[h] = acc[h, :, :D] * (1.0 / acc[h, :, D : D + 1])
        return 0

    lax.fori_loop(0, heads, finish, 0)


def finish(qf_ref, near_ref, mine_ref, other_ref, teacher_ref, student_ref, loss_ref, total):
    heads, tokens = qf_ref.shape[:2]
    lane = lax.broadcasted_iota(jnp.int32, (tokens, D), 1)
    total[...] = jnp.zeros_like(total)
    for h in range(heads):
        qf = qf_ref[h]
        far = mm(qf, jnp.concatenate([mine_ref[h], mine_ref[heads]], 1))
        far = far + mm(qf, jnp.concatenate([other_ref[h], other_ref[heads]], 1))
        picked = jnp.where((lane == h) | (lane == heads + h), far[:, D:], 0.0)
        below = near_ref[h, :, D : D + 1] + jnp.sum(picked, 1, keepdims=True)
        student = (near_ref[h, :, :D] + far[:, :D]) * (1.0 / below)
        student_ref[:, h * D : (h + 1) * D] = student.astype(BF16)
        total[...] += (student - teacher_ref[h]) ** 2
    per_token = jnp.sum(total[...].T, 0, keepdims=True) * (1.0 / HQ)
    blocks, width = loss_ref.shape
    t = lax.broadcasted_iota(jnp.int32, (blocks, tokens), 1)
    b = lax.broadcasted_iota(jnp.int32, (blocks, tokens), 0)
    own = (t >= b * width) & (t < (b + 1) * width)
    ti = lax.broadcasted_iota(jnp.int32, (tokens, width), 0)
    ji = lax.broadcasted_iota(jnp.int32, (tokens, width), 1)
    pick = jnp.zeros((tokens, width), F32)
    for i in range(blocks):
        pick = pick + (ti == ji + i * width).astype(F32)
    loss_ref[...] = jnp.dot(
        jnp.where(own, jnp.broadcast_to(per_token, (blocks, tokens)), 0.0),
        pick,
        precision=lax.Precision.HIGHEST,
        preferred_element_type=F32,
    )


def call(kernel, outs, scratch, name, us, *args, scalars=0):
    return pl.pallas_call(
        kernel,
        out_shape=outs,
        in_specs=[SMEM] * scalars + [VMEM] * (len(args) - scalars),
        out_specs=jax.tree.map(lambda _: VMEM, outs),
        scratch_shapes=scratch,
        name=name,
        cost_estimate=pl.CostEstimate(
            flops=int(us * 1e9), bytes_accessed=1 << 20, transcendentals=0
        ),
        compiler_params=pltpu.CompilerParams(vmem_limit_bytes=48 << 20),
    )(*args)


def shape(dims, dtype=F32):
    return jax.ShapeDtypeStruct(dims, dtype)


def shifted(x, axis, k):
    n = lax.axis_size(axis)
    return lax.ppermute(x, axis, [(i, (i + k) % n) for i in range(n)])


def body(queries, keys, values, feat_q, feat_k):
    tokens = queries.shape[0]
    heads = feat_q.shape[0]
    at = jnp.stack([lax.axis_index(a) for a in SEQ]).astype(jnp.int32)
    kv = jnp.concatenate([keys, values], 1)
    zs = [kv] + [shifted(kv, "z", k) for k in range(1, lax.axis_size("z"))]
    row = jnp.concatenate(zs, 0)
    half = row.shape[0]
    other = shifted(row, "c", 1)
    above = [shifted(row, "y", k) for k in range(1, lax.axis_size("y"))]
    above_other = [shifted(a, "c", 1) for a in above]

    qf, wk = call(
        prepare,
        (shape((heads, tokens, F), BF16), shape((heads, D, F), BF16)),
        [],
        "prepare",
        2,
        queries,
        feat_q,
        feat_k,
    )
    wide = [pltpu.VMEM((2 * half, F), BF16), pltpu.VMEM((2 * half, F), BF16)]
    acc0, m0, near = call(
        own_row,
        (shape((heads, tokens, F)), shape((heads, tokens, D)), shape((heads, tokens, F))),
        wide + [pltpu.VMEM((tokens, 2 * half), F32), pltpu.VMEM((tokens, 2 * half), F32)],
        "own_row",
        8,
        at,
        queries,
        qf,
        wk,
        row,
        other,
        scalars=1,
    )
    state = call(
        earlier_state,
        shape((heads + 1, F, D), BF16),
        [
            pltpu.VMEM((half, F), BF16),
            pltpu.VMEM((half, F), BF16),
            pltpu.VMEM((heads, F, F), F32),
            pltpu.VMEM((F, D), F32),
        ],
        "earlier_state",
        5,
        at,
        wk,
        *above,
        scalars=1,
    )
    state_other = shifted(state, "c", 1)
    pairs = [r for pair in zip(above, above_other) for r in pair]
    teacher = call(
        earlier_teacher,
        shape((heads, tokens, D)),
        wide + [pltpu.VMEM((heads, tokens, F), F32), pltpu.VMEM((heads, tokens, D), F32)],
        "earlier_teacher",
        8,
        at,
        queries,
        acc0,
        m0,
        *pairs,
        scalars=1,
    )
    parts = lax.axis_size("head")
    student, loss = call(
        finish,
        (shape((tokens, heads * D), BF16), shape((parts, tokens // parts))),
        [pltpu.VMEM((tokens, D), F32)],
        "finish",
        2,
        qf,
        near,
        state,
        state_other,
        teacher,
    )
    tiles = lax.all_to_all(loss[:, None, :], "head", 0, 0, tiled=True)
    return student, jnp.sum(tiles, axis=(0, 1))


def solution(mesh):
    grid = Mesh(mesh.devices.reshape(4, 4, 2, mesh.shape["head"]), (*SEQ, "head"))
    placed = P(SEQ, "head")
    return jax.shard_map(
        body,
        mesh=grid,
        in_specs=(placed, placed, placed, P("head"), P("head")),
        out_specs=(placed, P((*SEQ, "head"))),
        check_vma=False,
    )
```

```python
import math

import jax
import jax.numpy as jnp
from jax import lax
from jax.experimental import pallas as pl
from jax.experimental.pallas import tpu as pltpu
from jax.sharding import Mesh
from jax.sharding import PartitionSpec as P

HQ = 128
D = 128
F = 2 * D
LOG2E = math.log2(math.e)
SCALE = LOG2E / math.sqrt(D)
NEG = -1e30
SEQ = ("y", "z", "c")
F32, BF16 = jnp.float32, jnp.bfloat16
VMEM = pl.BlockSpec(memory_space=pltpu.VMEM)
SMEM = pl.BlockSpec(memory_space=pltpu.SMEM)


def mm(a, b):
    return jnp.dot(a, b, preferred_element_type=F32)


def mm_t(a, b):
    return lax.dot_general(a, b, (((1,), (1,)), ((), ())), preferred_element_type=F32)


def split(x):
    high = x.astype(BF16)
    return high, (x - high.astype(F32)).astype(BF16)


def both_softmax(x, axis):
    up = jnp.exp2(x - jnp.max(x, axis, keepdims=True))
    down = jnp.exp2(jnp.min(x, axis, keepdims=True) - x)
    up = up * (1.0 / jnp.sum(up, axis, keepdims=True))
    down = down * (1.0 / jnp.sum(down, axis, keepdims=True))
    return up.astype(BF16), down.astype(BF16)


def one_column(rows):
    return (lax.broadcasted_iota(jnp.int32, (rows, D), 1) == 0).astype(F32).astype(BF16)


def fill(k2_ref, v1_ref, at, kv):
    rows = kv.shape[0]
    k2_ref[at : at + rows, :D] = kv[:, :D]
    k2_ref[at : at + rows, D:] = kv[:, :D]
    v1_ref[at : at + rows, :D] = kv[:, D:]
    v1_ref[at : at + rows, D:] = one_column(rows)


def prepare(q_ref, fq_ref, fk_ref, q2_ref, qf_ref, wk_ref):
    tokens = q_ref.shape[0]

    def head(h, _):
        q = q_ref[:, pl.ds(pl.multiple_of(h * D, D), D)]
        rows = pl.ds(pl.multiple_of(h * tokens, tokens), tokens)
        high, low = split(q.astype(F32) * SCALE)
        q2_ref[rows, :D] = high
        q2_ref[rows, D:] = low
        up, down = both_softmax(mm(q, fq_ref[h]) * LOG2E, 1)
        qf_ref[h, :, :D] = up
        qf_ref[h, :, D:] = down
        high, low = split((fk_ref[h].astype(F32) * LOG2E).T)
        rows = pl.ds(pl.multiple_of(h * D, D), D)
        wk_ref[rows, :D] = high
        wk_ref[rows, D:] = low
        return 0

    lax.fori_loop(0, fq_ref.shape[0], head, 0, unroll=4)


def row_max(s):
    parts = [s[:, i : i + D] for i in range(0, s.shape[1], D)]
    while len(parts) > 1:
        parts = [jnp.maximum(a, b) for a, b in zip(parts[::2], parts[1::2])]
    return jnp.max(parts[0], 1, keepdims=True)


def own_row(at_ref, q2_ref, qf_ref, wk_ref, mine_ref, other_ref, acc_ref, m_ref, near_ref, k2, v1, bias, keep, s0, s1, x0, x1, f0, f1):
    heads, tokens = qf_ref.shape[:2]
    half = mine_ref.shape[0]
    z, c = at_ref[1], at_ref[2]
    fill(k2, v1, 0, mine_ref[...])
    fill(k2, v1, half, other_ref[...])
    row = lax.broadcasted_iota(jnp.int32, (tokens, tokens), 0)
    col = lax.broadcasted_iota(jnp.int32, (tokens, tokens), 1)
    for slot in range(half // tokens):
        for side in range(2):
            if slot == 0 and side == 0:
                seen = (col <= row).astype(F32)
            else:
                allowed = slot <= z if slot else c == 1
                seen = jnp.full((tokens, tokens), jnp.where(allowed, 1.0, 0.0), F32)
            at = side * half + slot * tokens
            keep[:, at : at + tokens] = seen
            bias[:, at : at + tokens] = (1.0 - seen) * NEG

    def first(h, s, x):
        s[...] = mm_t(q2_ref[pl.ds(pl.multiple_of(h * tokens, tokens), tokens)], k2[...]) + bias[...]
        x[...] = mm_t(wk_ref[pl.ds(pl.multiple_of(h * D, D), D)], k2[...])

    def second(h, s, x, f):
        rows = pl.ds(pl.multiple_of(h * tokens, tokens), tokens)
        m = row_max(s[...])
        p = jnp.exp2(s[...] - m).astype(BF16)
        up, down = both_softmax(x[...], 0)
        f[:D] = up
        f[D:] = down
        acc_ref[rows] = mm(p, v1[...])
        m_ref[rows] = jnp.broadcast_to(m, (tokens, D))

    def third(h, f):
        a = (mm(qf_ref[h], f[...]) * keep[...]).astype(BF16)
        near_ref[h] = mm(a, v1[...])

    first(0, s0, x0)
    f1[...] = jnp.zeros_like(f1)

    def step(i, _):
        h = 2 * i
        first(h + 1, s1, x1)
        second(h, s0, x0, f0)
        third(jnp.maximum(h - 1, 0), f1)
        first(jnp.minimum(h + 2, heads - 1), s0, x0)
        second(h + 1, s1, x1, f1)
        third(h, f0)
        return 0

    lax.fori_loop(0, heads // 2, step, 0)
    third(heads - 1, f1)


def earlier_state(at_ref, wk_ref, *refs):
    rows, (out_ref, k2, v1, state, sums, x0, x1, f0, f1) = refs[:-9], refs[-9:]
    heads = out_ref.shape[0] - 1
    half = rows[0].shape[0]
    pairs = heads // 2
    count = at_ref[0] * pairs
    state[...] = jnp.zeros_like(state)
    f1[...] = jnp.zeros_like(f1)
    for k, row_ref in enumerate(rows):

        @pl.when(at_ref[0] > k)
        def _(k=k, row_ref=row_ref):
            fill(k2, v1, k * half, row_ref[...])

    def place(t):
        t = jnp.clip(t, 0, jnp.maximum(count - 1, 0))
        k, pair = lax.div(t, pairs), lax.rem(t, pairs)
        return pl.ds(pl.multiple_of(k * half, half), half), pair

    def first(t, x):
        at, pair = place(t)
        x[...] = mm_t(wk_ref[pl.ds(pl.multiple_of(pair * 2 * D, 2 * D), 2 * D)], k2[at])

    def second(x, f):
        for i in range(2):
            up, down = both_softmax(x[i * D : (i + 1) * D], 0)
            f[i * F : i * F + D] = up
            f[i * F + D : (i + 1) * F] = down

    def third(t, f):
        at, pair = place(t)
        state[pl.ds(pl.multiple_of(pair * 2 * F, 2 * F), 2 * F)] += mm(f[...], v1[at])

    @pl.when(count > 0)
    def _():
        first(0, x0)

        def step(i, _):
            t = 2 * i
            first(t + 1, x1)
            second(x0, f0)
            third(t - 1, f1)
            first(t + 2, x0)
            second(x1, f1)
            third(t, f0)
            return 0

        lax.fori_loop(0, lax.div(count, 2), step, 0)
        third(count - 1, f1)

    lane = lax.broadcasted_iota(jnp.int32, (F, D), 1)
    sums[...] = jnp.zeros_like(sums)
    for h in range(heads):
        out_ref[h] = state[h * F : (h + 1) * F, :D].astype(BF16)
        total = state[h * F : (h + 1) * F, D : D + 1]
        sums[...] += jnp.where(lane == h, total, 0.0)
    high, low = split(sums[...])
    out_ref[heads] = (high.astype(F32) + pltpu.roll(low.astype(F32), heads, 1)).astype(BF16)


def earlier_teacher(at_ref, q2_ref, acc0_ref, m0_ref, *refs):
    rows, (acc, k2, v1, m_all, s0, s1, p0, p1) = refs[:-8], refs[-8:]
    half = rows[0].shape[0]
    wide = 2 * half
    part = s0.shape[0]
    groups = q2_ref.shape[0] // part
    count = at_ref[0] * groups
    m_all[...] = m0_ref[...]
    for k in range(len(rows) // 2):

        @pl.when(at_ref[0] > k)
        def _(k=k):
            fill(k2, v1, k * wide, rows[2 * k][...])
            fill(k2, v1, k * wide + half, rows[2 * k + 1][...])

    def place(t):
        t = jnp.clip(t, 0, jnp.maximum(count - 1, 0))
        k, g = lax.div(t, groups), lax.rem(t, groups)
        return pl.ds(pl.multiple_of(k * wide, wide), wide), pl.multiple_of(g * part, part)

    def first(t, s):
        at, g = place(t)
        s[...] = mm_t(q2_ref[pl.ds(g, part)], k2[at])

    def second(t, s, p):
        at, g = place(t)
        for i in range(0, part, D):
            here = pl.ds(pl.multiple_of(g + i, D), D)
            before = m_all[here]
            m = jnp.maximum(before, row_max(s[i : i + D]))
            m_all[here] = m
            factor = jnp.exp2(before - m)
            acc[here] = acc[here] * jnp.concatenate([factor, factor], 1)
            m = jnp.concatenate([m] * (wide // D), 1)
            p[i : i + D] = jnp.exp2(s[i : i + D] - m).astype(BF16)

    def third(t, p):
        at, g = place(t)
        acc[pl.ds(g, part)] += mm(p[...], v1[at])

    @pl.when(count > 0)
    def _():
        first(0, s0)

        def step(i, _):
            t = 2 * i
            first(t + 1, s1)
            second(t, s0, p0)
            third(t, p0)
            first(t + 2, s0)
            second(t + 1, s1, p1)
            third(t + 1, p1)
            return 0

        lax.fori_loop(0, lax.div(count, 2), step, 0)


def finish(qf_ref, near_ref, mine_ref, other_ref, acc_ref, student_ref, loss_ref, total):
    heads, tokens = qf_ref.shape[:2]
    lane = lax.broadcasted_iota(jnp.int32, (tokens, D), 1)
    total[...] = jnp.zeros_like(total)
    for h in range(heads):
        qf = qf_ref[h]
        far = mm(qf, jnp.concatenate([mine_ref[h], mine_ref[heads]], 1))
        far = far + mm(qf, jnp.concatenate([other_ref[h], other_ref[heads]], 1))
        picked = jnp.where((lane == h) | (lane == heads + h), far[:, D:], 0.0)
        below = near_ref[h, :, D : D + 1] + jnp.sum(picked, 1, keepdims=True)
        student = (near_ref[h, :, :D] + far[:, :D]) * (1.0 / below)
        student_ref[:, h * D : (h + 1) * D] = student.astype(BF16)
        acc = acc_ref[h * tokens : (h + 1) * tokens]
        teacher = acc[:, :D] * (1.0 / acc[:, D : D + 1])
        total[...] += (student - teacher) ** 2
    per_token = jnp.sum(total[...].T, 0, keepdims=True) * (1.0 / HQ)
    blocks, width = loss_ref.shape
    t = lax.broadcasted_iota(jnp.int32, (blocks, tokens), 1)
    b = lax.broadcasted_iota(jnp.int32, (blocks, tokens), 0)
    own = (t >= b * width) & (t < (b + 1) * width)
    ti = lax.broadcasted_iota(jnp.int32, (tokens, width), 0)
    ji = lax.broadcasted_iota(jnp.int32, (tokens, width), 1)
    pick = jnp.zeros((tokens, width), F32)
    for i in range(blocks):
        pick = pick + (ti == ji + i * width).astype(F32)
    loss_ref[...] = jnp.dot(
        jnp.where(own, jnp.broadcast_to(per_token, (blocks, tokens)), 0.0),
        pick,
        precision=lax.Precision.HIGHEST,
        preferred_element_type=F32,
    )


def call(kernel, outs, scratch, name, us, *args, scalars=0, aliases=None):
    return pl.pallas_call(
        kernel,
        out_shape=outs,
        in_specs=[SMEM] * scalars + [VMEM] * (len(args) - scalars),
        out_specs=jax.tree.map(lambda _: VMEM, outs),
        scratch_shapes=scratch,
        name=name,
        input_output_aliases=aliases or {},
        cost_estimate=pl.CostEstimate(
            flops=int(us * 1e9), bytes_accessed=1 << 20, transcendentals=0
        ),
        compiler_params=pltpu.CompilerParams(vmem_limit_bytes=48 << 20),
    )(*args)


def shape(dims, dtype=F32):
    return jax.ShapeDtypeStruct(dims, dtype)


def shifted(x, axis, k):
    n = lax.axis_size(axis)
    return lax.ppermute(x, axis, [(i, (i + k) % n) for i in range(n)])


def body(queries, keys, values, feat_q, feat_k):
    tokens = queries.shape[0]
    heads = feat_q.shape[0]
    depth = lax.axis_size("y")
    at = jnp.stack([lax.axis_index(a) for a in SEQ]).astype(jnp.int32)
    kv = jnp.concatenate([keys, values], 1)
    zs = [shifted(kv, "z", k) for k in range(1, lax.axis_size("z"))]
    q2, qf, wk = call(
        prepare,
        (shape((heads * tokens, F), BF16), shape((heads, tokens, F), BF16), shape((heads * D, F), BF16)),
        [],
        "prepare",
        3,
        queries,
        feat_q,
        feat_k,
    )
    zs, q2, qf, wk = lax.optimization_barrier((zs, q2, qf, wk))
    row = jnp.concatenate([kv, *zs], 0)
    half = row.shape[0]
    above = [shifted(row, "y", k) for k in range(1, depth)]
    other = shifted(row, "c", 1)
    acc0, m0, near = call(
        own_row,
        (shape((heads * tokens, F)), shape((heads * tokens, D)), shape((heads, tokens, F))),
        [
            pltpu.VMEM((2 * half, F), BF16),
            pltpu.VMEM((2 * half, F), BF16),
            pltpu.VMEM((tokens, 2 * half), F32),
            pltpu.VMEM((tokens, 2 * half), F32),
            pltpu.VMEM((tokens, 2 * half), F32),
            pltpu.VMEM((tokens, 2 * half), F32),
            pltpu.VMEM((D, 2 * half), F32),
            pltpu.VMEM((D, 2 * half), F32),
            pltpu.VMEM((F, 2 * half), BF16),
            pltpu.VMEM((F, 2 * half), BF16),
        ],
        "own_row",
        10,
        at,
        q2,
        qf,
        wk,
        row,
        other,
        scalars=1,
    )
    above, acc0, m0, near = lax.optimization_barrier((above, acc0, m0, near))
    above_other = [shifted(a, "c", 1) for a in above]
    earlier = (depth - 1) * half
    state = call(
        earlier_state,
        shape((heads + 1, F, D), BF16),
        [
            pltpu.VMEM((earlier, F), BF16),
            pltpu.VMEM((earlier, F), BF16),
            pltpu.VMEM((heads * F, F), F32),
            pltpu.VMEM((F, D), F32),
            pltpu.VMEM((2 * D, half), F32),
            pltpu.VMEM((2 * D, half), F32),
            pltpu.VMEM((2 * F, half), BF16),
            pltpu.VMEM((2 * F, half), BF16),
        ],
        "earlier_state",
        5,
        at,
        wk,
        *above,
        scalars=1,
    )
    state_other = shifted(state, "c", 1)
    pairs = [r for pair in zip(above, above_other) for r in pair]
    acc = call(
        earlier_teacher,
        shape((heads * tokens, F)),
        [
            pltpu.VMEM((2 * earlier, F), BF16),
            pltpu.VMEM((2 * earlier, F), BF16),
            pltpu.VMEM((heads * tokens, D), F32),
            pltpu.VMEM((4 * tokens, 2 * half), F32),
            pltpu.VMEM((4 * tokens, 2 * half), F32),
            pltpu.VMEM((4 * tokens, 2 * half), BF16),
            pltpu.VMEM((4 * tokens, 2 * half), BF16),
        ],
        "earlier_teacher",
        8,
        at,
        q2,
        acc0,
        m0,
        *pairs,
        scalars=1,
        aliases={2: 0},
    )
    parts = lax.axis_size("head")
    student, loss = call(
        finish,
        (shape((tokens, heads * D), BF16), shape((parts, tokens // parts))),
        [pltpu.VMEM((tokens, D), F32)],
        "finish",
        2,
        qf,
        near,
        state,
        state_other,
        acc,
    )
    tiles = lax.all_to_all(loss[:, None, :], "head", 0, 0, tiled=True)
    return student, jnp.sum(tiles, axis=(0, 1))


def solution(mesh):
    grid = Mesh(mesh.devices.reshape(4, 4, 2, mesh.shape["head"]), (*SEQ, "head"))
    placed = P(SEQ, "head")
    return jax.shard_map(
        body,
        mesh=grid,
        in_specs=(placed, placed, placed, P("head"), P("head")),
        out_specs=(placed, P((*SEQ, "head"))),
        check_vma=False,
    )
```

```python
import math

import jax
import jax.numpy as jnp
from jax import lax
from jax.experimental import pallas as pl
from jax.experimental.pallas import tpu as pltpu
from jax.sharding import Mesh
from jax.sharding import PartitionSpec as P


HQ = 128
D = 128
F = 2 * D
LOG2E = math.log2(math.e)
SCALE = LOG2E / math.sqrt(D)
NEG = -1e30
SEQ = ("y", "z", "c")
F32, BF16 = jnp.float32, jnp.bfloat16
VMEM = pl.BlockSpec(memory_space=pltpu.VMEM)
SMEM = pl.BlockSpec(memory_space=pltpu.SMEM)
ANY = pl.BlockSpec(memory_space=pl.ANY)
HBM = pl.BlockSpec(memory_space=pltpu.HBM)


def mm(a, b):
    return jnp.dot(a, b, preferred_element_type=F32)


def mm_t(a, b):
    return lax.dot_general(a, b, (((1,), (1,)), ((), ())), preferred_element_type=F32)


def split(x):
    high = x.astype(BF16)
    return high, (x - high.astype(F32)).astype(BF16)


def both_softmax(x, axis):
    up = jnp.exp2(x - jnp.max(x, axis, keepdims=True))
    down = jnp.exp2(jnp.min(x, axis, keepdims=True) - x)
    up = up * (1.0 / jnp.sum(up, axis, keepdims=True))
    down = down * (1.0 / jnp.sum(down, axis, keepdims=True))
    return up.astype(BF16), down.astype(BF16)


def fill(k2_ref, v1_ref, at, kv):
    rows = kv.shape[0]
    k2_ref[at : at + rows, :D] = kv[:, :D]
    k2_ref[at : at + rows, D:] = kv[:, :D]
    v1_ref[at : at + rows, :D] = kv[:, D:]
    v1_ref[at : at + rows, D:] = jnp.ones((rows, D), BF16)


def prepare(q_ref, fq_ref, fk_ref, q2_ref, qf_ref, wk_ref, wk_later_ref):
    tokens = q_ref.shape[0]

    def head(h, _):
        q = q_ref[:, pl.ds(pl.multiple_of(h * D, D), D)]
        rows = pl.ds(pl.multiple_of(h * tokens, tokens), tokens)
        high, low = split(q.astype(F32) * SCALE)
        q2_ref[rows, :D] = high
        q2_ref[rows, D:] = low
        up, down = both_softmax(mm(q, fq_ref[h]) * LOG2E, 1)
        qf_ref[rows, :D] = up
        qf_ref[rows, D:] = down
        high, low = split((fk_ref[h].astype(F32) * LOG2E).T)
        rows = pl.ds(pl.multiple_of(h * D, D), D)
        for ref in (wk_ref, wk_later_ref):
            ref[rows, :D] = high
            ref[rows, D:] = low
        return 0

    lax.fori_loop(0, fq_ref.shape[0], head, 0, unroll=4)


def lane_blocks(s):
    return [s[:, i : i + D] for i in range(0, s.shape[1], D)]


def row_max(parts):
    while len(parts) > 1:
        parts = [jnp.maximum(a, b) for a, b in zip(parts[::2], parts[1::2])]
    return jnp.max(parts[0], 1, keepdims=True)


def own_row(at_ref, q2_ref, qf_ref, wk_ref, mine_ref, other_ref, acc_ref, m_ref, near_ref, k2, v1, bias, keep, s0, s1, x0, x1, f0, f1, p0, p1, a0, a1):
    tokens = keep.shape[0]
    heads = qf_ref.shape[0] // tokens
    half = mine_ref.shape[0]
    wide = k2.shape[0]
    many = s0.shape[0] // tokens
    groups = heads // many
    tile = wide // many
    z, c = at_ref[1], at_ref[2]
    safe = jnp.broadcast_to(mine_ref[:16, :D].astype(F32)[:1], (tokens, D))
    for side, ref in enumerate((mine_ref, other_ref)):
        for slot in range(half // tokens):
            kv = ref[slot * tokens : (slot + 1) * tokens].astype(F32)
            key, value, one = kv[:, :D], kv[:, D:], jnp.ones((tokens, D), F32)
            if slot or side:
                seen = slot <= z if slot else c == 1
                key = jnp.where(seen, key, safe)
                value = jnp.where(seen, value, 0.0)
                one = jnp.where(seen, one, 0.0)
            here = slice(side * half + slot * tokens, side * half + (slot + 1) * tokens)
            k2[here, :D] = key.astype(BF16)
            k2[here, D:] = key.astype(BF16)
            v1[here, :D] = value.astype(BF16)
            v1[here, D:] = one.astype(BF16)
    row = lax.broadcasted_iota(jnp.int32, (tokens, tokens), 0)
    col = lax.broadcasted_iota(jnp.int32, (tokens, tokens), 1)
    seen = (col <= row).astype(F32)
    keep[...] = seen
    bias[...] = (1.0 - seen) * NEG

    def block(g, size):
        return pl.ds(pl.multiple_of(g * size, size), size)

    def first(g, s, x, j):
        cols = slice(j * tile, (j + 1) * tile)
        s[:, cols] = mm_t(q2_ref[block(g, many * tokens)], k2[cols])
        x[:, cols] = mm_t(wk_ref[block(g, many * D)], k2[cols])

    def second(g, s, x, p, f, i):
        here = slice(i * tokens, (i + 1) * tokens)
        parts = lane_blocks(s[here])
        parts[0] = parts[0] + bias[...]
        m = row_max(parts)
        m_ref[block(g * many + i, tokens)] = jnp.broadcast_to(m, (tokens, D))
        p[here] = jnp.concatenate([jnp.exp2(a - m).astype(BF16) for a in parts], 1)
        up, down = both_softmax(x[i * D : (i + 1) * D], 0)
        f[i * F : i * F + D] = up
        f[i * F + D : (i + 1) * F] = down

    def third(g, f, a, i):
        here = slice(i * tokens, (i + 1) * tokens)
        scores = mm(qf_ref[block(g * many + i, tokens)], f[i * F : (i + 1) * F])
        a[here, :D] = (scores[:, :D] * keep[...]).astype(BF16)
        a[here, D:] = scores[:, D:].astype(BF16)

    def mix(out_ref, g, p):
        out_ref[block(g, many * tokens)] = mm(p[...], v1[...])

    def stage(g, s, x, p, f, s_next, x_next, p_last, f_last, a_last, a_older):
        last, older = jnp.maximum(g - 1, 0), jnp.maximum(g - 2, 0)
        for j in range(many):
            first(jnp.minimum(g + 1, groups - 1), s_next, x_next, j)
            second(g, s, x, p, f, j)
            third(last, f_last, a_last, j)
            if j == 0:
                mix(acc_ref, last, p_last)
            if j == 2:
                mix(near_ref, older, a_older)

    for j in range(many):
        first(0, s0, x0, j)
    f1[...] = jnp.zeros_like(f1)
    p1[...] = jnp.zeros_like(p1)
    a0[...] = jnp.zeros_like(a0)

    def step(i, _):
        g = 2 * i
        stage(g, s0, x0, p0, f0, s1, x1, p1, f1, a1, a0)
        stage(g + 1, s1, x1, p1, f1, s0, x0, p0, f0, a0, a1)
        return 0

    lax.fori_loop(0, groups // 2, step, 0)
    mix(acc_ref, groups - 1, p1)
    mix(near_ref, groups - 2, a0)
    for j in range(many):
        third(groups - 1, f1, a1, j)
    mix(near_ref, groups - 1, a1)


def earlier_state(at_ref, wk_ref, *refs):
    rows, (out_ref, k2, v1, state, x0, x1, f0, f1) = refs[:-8], refs[-8:]
    heads = out_ref.shape[0] // F
    half = rows[0].shape[0]
    pairs = heads // 2
    count = at_ref[0] * pairs
    state[...] = jnp.zeros_like(state)
    f1[...] = jnp.zeros_like(f1)
    for k, row_ref in enumerate(rows):

        @pl.when(at_ref[0] > k)
        def _(k=k, row_ref=row_ref):
            fill(k2, v1, k * half, row_ref[...])

    def place(t):
        t = jnp.clip(t, 0, jnp.maximum(count - 1, 0))
        k, pair = lax.div(t, pairs), lax.rem(t, pairs)
        return pl.ds(pl.multiple_of(k * half, half), half), pair

    def first(t, x):
        at, pair = place(t)
        x[...] = mm_t(wk_ref[pl.ds(pl.multiple_of(pair * 2 * D, 2 * D), 2 * D)], k2[at])

    def second(x, f):
        for i in range(2):
            up, down = both_softmax(x[i * D : (i + 1) * D], 0)
            f[i * F : i * F + D] = up
            f[i * F + D : (i + 1) * F] = down

    def third(t, f):
        at, pair = place(t)
        state[pl.ds(pl.multiple_of(pair * 2 * F, 2 * F), 2 * F)] += mm(f[...], v1[at])

    @pl.when(count > 0)
    def _():
        first(0, x0)

        def step(i, _):
            t = 2 * i
            first(t + 1, x1)
            second(x0, f0)
            third(t - 1, f1)
            first(t + 2, x0)
            second(x1, f1)
            third(t, f0)
            return 0

        lax.fori_loop(0, lax.div(count, 2), step, 0)
        third(count - 1, f1)

    out_ref[...] = state[...].astype(BF16)


def earlier_teacher(at_ref, q2_ref, acc0_ref, m0_ref, *refs):
    rows, (acc, k2, v1, m_all, s0, s1, p0, p1) = refs[:-8], refs[-8:]
    half = rows[0].shape[0]
    wide = 2 * half
    part = s0.shape[0]
    groups = q2_ref.shape[0] // part
    count = at_ref[0] * groups
    m_all[...] = m0_ref[...]
    for k in range(len(rows) // 2):

        @pl.when(at_ref[0] > k)
        def _(k=k):
            fill(k2, v1, k * wide, rows[2 * k][...])
            fill(k2, v1, k * wide + half, rows[2 * k + 1][...])

    def place(t):
        t = jnp.clip(t, 0, jnp.maximum(count - 1, 0))
        k, g = lax.div(t, groups), lax.rem(t, groups)
        return pl.ds(pl.multiple_of(k * wide, wide), wide), pl.multiple_of(g * part, part)

    def first(t, s):
        at, g = place(t)
        s[...] = mm_t(q2_ref[pl.ds(g, part)], k2[at])

    def second(t, s, p):
        _, g = place(t)
        for i in range(0, part, D):
            here = pl.ds(pl.multiple_of(g + i, D), D)
            before = m_all[here]
            m = jnp.maximum(before, row_max(lane_blocks(s[i : i + D])))
            m_all[here] = m
            factor = jnp.exp2(before - m)
            acc[here] = acc[here] * jnp.concatenate([factor, factor], 1)
            m = jnp.concatenate([m] * (wide // D), 1)
            p[i : i + D] = jnp.exp2(s[i : i + D] - m).astype(BF16)

    def third(t, p):
        at, g = place(t)
        acc[pl.ds(g, part)] += mm(p[...], v1[at])

    @pl.when(count > 0)
    def _():
        first(0, s0)

        def step(i, _):
            t = 2 * i
            first(t + 1, s1)
            second(t, s0, p0)
            third(t, p0)
            first(t + 2, s0)
            second(t + 1, s1, p1)
            third(t + 1, p1)
            return 0

        lax.fori_loop(0, lax.div(count, 2), step, 0)


def finish(qf_ref, near_ref, mine_ref, other_ref, acc_ref, student_ref, loss_ref, total, out, sems):
    tokens = total.shape[0]
    heads = qf_ref.shape[0] // tokens
    many = heads // sems.shape[0]
    total[...] = jnp.zeros_like(total)
    copies = []
    for h in range(heads):
        here = slice(h * tokens, (h + 1) * tokens)
        there = slice(h * F, (h + 1) * F)
        qf = qf_ref[here]
        sums = near_ref[here] + mm(qf, mine_ref[there]) + mm(qf, other_ref[there])
        student = sums[:, :D] * (1.0 / sums[:, D:])
        out[:, h * D : (h + 1) * D] = student.astype(BF16)
        acc = acc_ref[here]
        total[...] += (student - acc[:, :D] * (1.0 / acc[:, D:])) ** 2
        if (h + 1) % many == 0:
            i = h // many
            cols = slice(i * many * D, (i + 1) * many * D)
            copies.append(pltpu.make_async_copy(out.at[:, cols], student_ref.at[:, cols], sems.at[i]))
            copies[-1].start()
    per_token = jnp.sum(total[...].T, 0, keepdims=True) * (1.0 / HQ)
    blocks, width = loss_ref.shape
    t = lax.broadcasted_iota(jnp.int32, (blocks, tokens), 1)
    b = lax.broadcasted_iota(jnp.int32, (blocks, tokens), 0)
    own = (t >= b * width) & (t < (b + 1) * width)
    ti = lax.broadcasted_iota(jnp.int32, (tokens, width), 0)
    ji = lax.broadcasted_iota(jnp.int32, (tokens, width), 1)
    pick = jnp.zeros((tokens, width), F32)
    for i in range(blocks):
        pick = pick + (ti == ji + i * width).astype(F32)
    loss_ref[...] = jnp.dot(
        jnp.where(own, jnp.broadcast_to(per_token, (blocks, tokens)), 0.0),
        pick,
        precision=lax.Precision.HIGHEST,
        preferred_element_type=F32,
    )
    for copy in copies:
        copy.wait()


def pack(keys_ref, values_ref, kv_ref, sems):
    copies = [
        pltpu.make_async_copy(src, kv_ref.at[:, i * D : (i + 1) * D], sems.at[i])
        for i, src in enumerate((keys_ref, values_ref))
    ]
    for copy in copies:
        copy.start()
    for copy in copies:
        copy.wait()


def call(kernel, outs, scratch, us, mib, *args, scalars=0, aliases=None, ins=None, spec=None):
    return pl.pallas_call(
        kernel,
        out_shape=outs,
        in_specs=ins or [SMEM] * scalars + [VMEM] * (len(args) - scalars),
        out_specs=spec or jax.tree.map(lambda _: VMEM, outs),
        scratch_shapes=scratch,
        input_output_aliases=aliases or {},
        cost_estimate=pl.CostEstimate(
            flops=int(us * 1e9), bytes_accessed=1 << 20, transcendentals=0
        ),
        compiler_params=pltpu.CompilerParams(vmem_limit_bytes=mib << 20),
    )(*args)


def shape(dims, dtype=F32):
    return jax.ShapeDtypeStruct(dims, dtype)


def shifted(x, axis, k):
    n = lax.axis_size(axis)
    return lax.ppermute(x, axis, [(i, (i + k) % n) for i in range(n)])


def body(queries, keys, values, feat_q, feat_k):
    tokens = queries.shape[0]
    heads = feat_q.shape[0]
    depth = lax.axis_size("y")
    at = jnp.stack([lax.axis_index(a) for a in SEQ]).astype(jnp.int32)
    rows = heads * tokens
    kv = call(
        pack,
        shape((tokens, F), BF16),
        [pltpu.SemaphoreType.DMA((2,))],
        1,
        1,
        keys,
        values,
        ins=[HBM, HBM],
    )
    zs = [shifted(kv, "z", k) for k in range(1, lax.axis_size("z"))]
    q2, qf, wk, wk_later = call(
        prepare,
        (shape((rows, F), BF16),) * 2 + (shape((heads * D, F), BF16),) * 2,
        [],
        3,
        10,
        queries,
        feat_q,
        feat_k,
    )
    zs, q2, qf, wk = lax.optimization_barrier((zs, q2, qf, wk))
    row = jnp.concatenate([kv, *zs], 0)
    half = row.shape[0]
    above = [shifted(row, "y", k) for k in range(1, depth)]
    other = shifted(row, "c", 1)
    many = 4
    acc0, m0, near = call(
        own_row,
        (shape((rows, F)), shape((rows, D)), shape((rows, F))),
        [pltpu.VMEM((2 * half, F), BF16)] * 2
        + [pltpu.VMEM((tokens, tokens), F32)] * 2
        + [pltpu.VMEM((many * tokens, 2 * half), F32)] * 4
        + [pltpu.VMEM((many * F, 2 * half), BF16)] * 2
        + [pltpu.VMEM((many * tokens, 2 * half), BF16)] * 4,
        10,
        30,
        at,
        q2,
        qf,
        wk,
        row,
        other,
        scalars=1,
    )
    above, acc0, m0, near = lax.optimization_barrier((above, acc0, m0, near))
    above_other = []
    for a in above:
        above_other.append(shifted(a, "c", 1))
    earlier = (depth - 1) * half
    state = call(
        earlier_state,
        shape((heads * F, F), BF16),
        [pltpu.VMEM((earlier, F), BF16)] * 2
        + [pltpu.VMEM((heads * F, F), F32)]
        + [pltpu.VMEM((2 * D, half), F32)] * 2
        + [pltpu.VMEM((2 * F, half), BF16)] * 2,
        5,
        14,
        at,
        wk_later,
        *above,
        scalars=1,
    )
    state_other = shifted(state, "c", 1)
    pairs = [r for pair in zip(above, above_other) for r in pair]
    acc = call(
        earlier_teacher,
        shape((rows, F)),
        [pltpu.VMEM((2 * earlier, F), BF16)] * 2
        + [pltpu.VMEM((rows, D), F32)]
        + [pltpu.VMEM((many * tokens, 2 * half), F32)] * 2
        + [pltpu.VMEM((many * tokens, 2 * half), BF16)] * 2,
        8,
        18,
        at,
        q2,
        acc0,
        m0,
        *pairs,
        scalars=1,
        aliases={2: 0},
    )
    parts = lax.axis_size("head")
    student, loss = call(
        finish,
        (shape((tokens, heads * D), BF16), shape((parts, tokens // parts))),
        [
            pltpu.VMEM((tokens, D), F32),
            pltpu.VMEM((tokens, heads * D), BF16),
            pltpu.SemaphoreType.DMA((4,)),
        ],
        2,
        14,
        qf,
        near,
        state,
        state_other,
        acc,
        spec=(ANY, VMEM),
    )
    tiles = lax.all_to_all(loss[:, None, :], "head", 0, 0, tiled=True)
    return student, jnp.sum(tiles, axis=(0, 1))


def solution(mesh):
    grid = Mesh(mesh.devices.reshape(4, 4, 2, mesh.shape["head"]), (*SEQ, "head"))
    placed = P(SEQ, "head")
    return jax.shard_map(
        body,
        mesh=grid,
        in_specs=(placed, placed, placed, P("head"), P("head")),
        out_specs=(placed, P((*SEQ, "head"))),
        check_vma=False,
    )
```

```python
import functools
import math

import jax
import jax.numpy as jnp
from jax import lax
from jax.experimental import pallas as pl
from jax.experimental.pallas import tpu as pltpu
from jax.sharding import Mesh
from jax.sharding import PartitionSpec as P


HQ = 128
D = 128
F = 2 * D
LOG2E = math.log2(math.e)
SCALE = LOG2E / math.sqrt(D)
NEG = -1e30
MOST = 67043328
SEQ = ("y", "z", "c")
F32, BF16 = jnp.float32, jnp.bfloat16
VMEM = pl.BlockSpec(memory_space=pltpu.VMEM)
SMEM = pl.BlockSpec(memory_space=pltpu.SMEM)
ANY = pl.BlockSpec(memory_space=pl.ANY)
HBM = pl.BlockSpec(memory_space=pltpu.HBM)


def mm(a, b):
    return jnp.dot(a, b, preferred_element_type=F32)


def mm_t(a, b):
    return lax.dot_general(a, b, (((1,), (1,)), ((), ())), preferred_element_type=F32)


def split(x):
    high = x.astype(BF16)
    return high, (x - high.astype(F32)).astype(BF16)


def both_softmax(x, axis):
    up = jnp.exp2(x - jnp.max(x, axis, keepdims=True))
    down = jnp.exp2(jnp.min(x, axis, keepdims=True) - x)
    up = up * (1.0 / jnp.sum(up, axis, keepdims=True))
    down = down * (1.0 / jnp.sum(down, axis, keepdims=True))
    return up.astype(BF16), down.astype(BF16)


def prepare(start, q_ref, fq_ref, q2_ref, qf_ref):
    tokens = q_ref.shape[0]

    def head(h, _):
        q = q_ref[:, pl.ds(pl.multiple_of(h * D, D), D)]
        rows = pl.ds(pl.multiple_of(h * tokens, tokens), tokens)
        high, low = split(q.astype(F32) * SCALE)
        q2_ref[rows, :D] = high
        q2_ref[rows, D:] = low
        up, down = both_softmax(mm(q, fq_ref[start + h]) * LOG2E, 1)
        qf_ref[rows, :D] = up
        qf_ref[rows, D:] = down
        return 0

    lax.fori_loop(0, q2_ref.shape[0] // tokens, head, 0, unroll=4)


def prepare_keys(fk_ref, wk_ref):
    def head(h, _):
        high, low = split((fk_ref[h].astype(F32) * LOG2E).T)
        rows = pl.ds(pl.multiple_of(h * D, D), D)
        wk_ref[rows, :D] = high
        wk_ref[rows, D:] = low
        return 0

    lax.fori_loop(0, fk_ref.shape[0], head, 0, unroll=4)


def lane_blocks(s):
    return [s[:, i : i + D] for i in range(0, s.shape[1], D)]


def row_max(parts):
    while len(parts) > 1:
        parts = [jnp.maximum(a, b) for a, b in zip(parts[::2], parts[1::2])]
    return jnp.max(parts[0], 1, keepdims=True)


def own_row(start, at_ref, q2_ref, qf_ref, wk_ref, *refs):
    rows, refs = refs[:-17], refs[-17:]
    acc_ref, m_ref, near_ref, k2, v1, bias, keep = refs[:7]
    s0, s1, x0, x1, f0, f1, p0, p1, a0, a1 = refs[7:]
    tokens = keep.shape[0]
    heads = qf_ref.shape[0] // tokens
    half = rows[0].shape[0]
    wide = k2.shape[0]
    many = s0.shape[0] // tokens
    groups = heads // many
    tile = wide // many
    z, c = at_ref[1], at_ref[2]
    safe = jnp.broadcast_to(rows[0][:16, :D].astype(F32)[:1], (tokens, D))
    for side, ref in enumerate(rows):
        for slot in range(half // tokens):
            kv = ref[slot * tokens : (slot + 1) * tokens].astype(F32)
            key, value, one = kv[:, :D], kv[:, D:], jnp.ones((tokens, D), F32)
            if slot or side:
                seen = slot <= z if slot else c == 1
                key = jnp.where(seen, key, safe)
                value = jnp.where(seen, value, 0.0)
                one = jnp.where(seen, one, 0.0)
            here = slice(side * half + slot * tokens, side * half + (slot + 1) * tokens)
            k2[here, :D] = key.astype(BF16)
            k2[here, D:] = key.astype(BF16)
            v1[here, :D] = value.astype(BF16)
            v1[here, D:] = one.astype(BF16)
    row = lax.broadcasted_iota(jnp.int32, (tokens, tokens), 0)
    col = lax.broadcasted_iota(jnp.int32, (tokens, tokens), 1)
    seen = (col <= row).astype(F32)
    keep[...] = seen
    bias[...] = (1.0 - seen) * NEG

    def block(g, size):
        return pl.ds(pl.multiple_of(g * size, size), size)

    def first(g, s, x, j):
        cols = slice(j * tile, (j + 1) * tile)
        s[:, cols] = mm_t(q2_ref[block(g, many * tokens)], k2[cols])
        x[:, cols] = mm_t(wk_ref[block(start // many + g, many * D)], k2[cols])

    def second(g, s, x, p, f, i):
        here = slice(i * tokens, (i + 1) * tokens)
        parts = lane_blocks(s[here])
        parts[0] = parts[0] + bias[...]
        m = row_max(parts)
        m_ref[block(g * many + i, tokens)] = jnp.broadcast_to(m, (tokens, D))
        p[here] = jnp.concatenate([jnp.exp2(a - m).astype(BF16) for a in parts], 1)
        up, down = both_softmax(x[i * D : (i + 1) * D], 0)
        f[i * F : i * F + D] = up
        f[i * F + D : (i + 1) * F] = down

    def third(g, f, a, i):
        here = slice(i * tokens, (i + 1) * tokens)
        scores = mm(qf_ref[block(g * many + i, tokens)], f[i * F : (i + 1) * F])
        a[here, :D] = (scores[:, :D] * keep[...]).astype(BF16)
        a[here, D:] = scores[:, D:].astype(BF16)

    def mix(out_ref, g, p):
        out_ref[block(g, many * tokens)] = mm(p[...], v1[...])

    def stage(g, s, x, p, f, s_next, x_next, p_last, f_last, a_last, a_older):
        last, older = jnp.maximum(g - 1, 0), jnp.maximum(g - 2, 0)
        for j in range(many):
            first(jnp.minimum(g + 1, groups - 1), s_next, x_next, j)
            second(g, s, x, p, f, j)
            third(last, f_last, a_last, j)
            if j == 0:
                mix(acc_ref, last, p_last)
            if j == many // 2:
                mix(near_ref, older, a_older)

    for j in range(many):
        first(0, s0, x0, j)
    f1[...] = jnp.zeros_like(f1)
    p1[...] = jnp.zeros_like(p1)
    a0[...] = jnp.zeros_like(a0)

    def step(i, _):
        g = 2 * i
        stage(g, s0, x0, p0, f0, s1, x1, p1, f1, a1, a0)
        stage(g + 1, s1, x1, p1, f1, s0, x0, p0, f0, a0, a1)
        return 0

    lax.fori_loop(0, groups // 2, step, 0)
    mix(acc_ref, groups - 1, p1)
    mix(near_ref, groups - 2, a0)
    for j in range(many):
        third(groups - 1, f1, a1, j)
    mix(near_ref, groups - 1, a1)


def absolute(at_ref, rows, store):
    depth = len(rows)
    y = at_ref[0]
    places = (y, depth - 1 - y, y + 1 - 2 * lax.rem(y, 2), lax.rem(y + depth // 2, depth))
    for r, refs in zip(places, rows):

        @pl.when(r < depth - 1)
        def _(r=r, refs=refs):
            store(r, refs)


def fill_at(k2, v1, at, size, kv):
    here = pl.ds(pl.multiple_of(at, size), size)
    k2[here, :D] = kv[:, :D]
    k2[here, D:] = kv[:, :D]
    v1[here, :D] = kv[:, D:]
    v1[here, D:] = jnp.ones((size, D), BF16)


def unit_of(at_ref, u, half_heads):
    mine = u < at_ref[0]
    return jnp.where(mine, u, u - at_ref[0]), jnp.where(mine, 0, half_heads)


def earlier_state(at_ref, wk_ref, *refs):
    rows, (out_ref, k2, v1, state, x0, x1, f0, f1) = refs[:-8], refs[-8:]
    heads = out_ref.shape[0] // F
    half = rows[0].shape[0]
    pairs = heads // 4
    count = (len(rows) - 1) * pairs
    state[...] = jnp.zeros_like(state)
    f1[...] = jnp.zeros_like(f1)
    absolute(at_ref, rows, lambda r, ref: fill_at(k2, v1, r * half, half, ref[...]))

    def place(t):
        t = jnp.clip(t, 0, count - 1)
        r, head = unit_of(at_ref, lax.div(t, pairs), heads // 2)
        head = head + 2 * lax.rem(t, pairs)
        return pl.ds(pl.multiple_of(r * half, half), half), head

    def first(t, x):
        at, head = place(t)
        x[...] = mm_t(wk_ref[pl.ds(pl.multiple_of(head * D, 2 * D), 2 * D)], k2[at])

    def second(x, f):
        for i in range(2):
            up, down = both_softmax(x[i * D : (i + 1) * D], 0)
            f[i * F : i * F + D] = up
            f[i * F + D : (i + 1) * F] = down

    def third(t, f):
        at, head = place(t)
        state[pl.ds(pl.multiple_of(head * F, 2 * F), 2 * F)] += mm(f[...], v1[at])

    first(0, x0)

    def step(i, _):
        t = 2 * i
        first(t + 1, x1)
        second(x0, f0)
        third(t - 1, f1)
        first(t + 2, x0)
        second(x1, f1)
        third(t, f0)
        return 0

    lax.fori_loop(0, count // 2, step, 0)
    third(count - 1, f1)
    out_ref[...] = state[...].astype(BF16)


def earlier_teacher(at_ref, q2a_ref, q2b_ref, acca_ref, accb_ref, ma_ref, mb_ref, *refs):
    rows, (acc, k2, v1, q2, m_all, s0, s1, p0, p1) = refs[:-9], refs[-9:]
    half = rows[0].shape[0]
    wide = 2 * half
    part = s0.shape[0]
    side = q2a_ref.shape[0]
    groups = side // part
    pairs = [rows[i : i + 2] for i in range(0, len(rows), 2)]
    count = (len(pairs) - 1) * groups
    for i, (q2_ref, acc_ref, m_ref) in enumerate(
        ((q2a_ref, acca_ref, ma_ref), (q2b_ref, accb_ref, mb_ref))
    ):
        here = slice(i * side, (i + 1) * side)
        q2[here] = q2_ref[...]
        acc[here] = acc_ref[...]
        m_all[here] = m_ref[...]

    def store(r, pair):
        for i, ref in enumerate(pair):
            fill_at(k2, v1, r * wide + i * half, half, ref[...])

    absolute(at_ref, pairs, store)

    def place(t):
        t = jnp.clip(t, 0, count - 1)
        r, at = unit_of(at_ref, lax.div(t, groups), side)
        at = pl.multiple_of(at + lax.rem(t, groups) * part, part)
        return pl.ds(pl.multiple_of(r * wide, wide), wide), at

    def first(t, s):
        at, g = place(t)
        s[...] = mm_t(q2[pl.ds(g, part)], k2[at])

    def second(t, s, p):
        _, g = place(t)
        for i in range(0, part, D):
            here = pl.ds(pl.multiple_of(g + i, D), D)
            before = m_all[here]
            m = jnp.maximum(before, row_max(lane_blocks(s[i : i + D])))
            m_all[here] = m
            factor = jnp.exp2(before - m)
            acc[here] = acc[here] * jnp.concatenate([factor, factor], 1)
            m = jnp.concatenate([m] * (wide // D), 1)
            p[i : i + D] = jnp.exp2(s[i : i + D] - m).astype(BF16)

    def third(t, p):
        at, g = place(t)
        acc[pl.ds(g, part)] += mm(p[...], v1[at])

    first(0, s0)

    def step(i, _):
        t = 2 * i
        first(t + 1, s1)
        second(t, s0, p0)
        third(t, p0)
        first(t + 2, s0)
        second(t + 1, s1, p1)
        third(t + 1, p1)
        return 0

    lax.fori_loop(0, count // 2, step, 0)


def by_place(total, blocks, width):
    tokens = total.shape[0]
    per_token = jnp.sum(total.T, 0, keepdims=True) * (1.0 / HQ)
    t = lax.broadcasted_iota(jnp.int32, (blocks, tokens), 1)
    b = lax.broadcasted_iota(jnp.int32, (blocks, tokens), 0)
    own = (t >= b * width) & (t < (b + 1) * width)
    ti = lax.broadcasted_iota(jnp.int32, (tokens, width), 0)
    ji = lax.broadcasted_iota(jnp.int32, (tokens, width), 1)
    pick = jnp.zeros((tokens, width), F32)
    for i in range(blocks):
        pick = pick + (ti == ji + i * width).astype(F32)
    return jnp.dot(
        jnp.where(own, jnp.broadcast_to(per_token, (blocks, tokens)), 0.0),
        pick,
        precision=lax.Precision.HIGHEST,
        preferred_element_type=F32,
    )


def finish(start, qf_ref, near_ref, mine_ref, other_ref, acc_ref, out_ref, loss_ref, total):
    tokens = total.shape[0]
    total[...] = jnp.zeros_like(total)
    for h in range(qf_ref.shape[0] // tokens):
        here = slice(h * tokens, (h + 1) * tokens)
        there = slice((start + h) * F, (start + h + 1) * F)
        qf = qf_ref[here]
        sums = near_ref[here] + mm(qf, mine_ref[there]) + mm(qf, other_ref[there])
        student = sums[:, :D] * (1.0 / sums[:, D:])
        out_ref[:, h * D : (h + 1) * D] = student.astype(BF16)
        acc = acc_ref[(start + h) * tokens : (start + h + 1) * tokens]
        total[...] += (student - acc[:, :D] * (1.0 / acc[:, D:])) ** 2
    loss_ref[...] = by_place(total[...], *loss_ref.shape)


def finish_mine(qf_ref, near_ref, mine_ref, other_ref, acc_ref, student_ref, loss_ref, total, out, sem):
    finish(0, qf_ref, near_ref, mine_ref, other_ref, acc_ref, out, loss_ref, total)
    copy = pltpu.make_async_copy(out, student_ref.at[:, : out.shape[1]], sem)
    copy.start()
    copy.wait()


def move(pairs, sems):
    copies = [pltpu.make_async_copy(a, b, sems.at[i]) for i, (a, b) in enumerate(pairs)]
    for copy in copies:
        copy.start()
    for copy in copies:
        copy.wait()


def stack(*refs):
    size = refs[0].shape[0]
    for i, ref in enumerate(refs[:-1]):
        refs[-1][i * size : (i + 1) * size] = ref[...]


def pack(at_ref, keys_ref, values_ref, kv_ref, sems):
    move(((keys_ref, kv_ref.at[:, :D]), (values_ref, kv_ref.at[:, D:])), sems)


def halve(q_ref, part_ref):
    part_ref[...] = q_ref[:, part_ref.shape[1] :]


def join(back_ref, student_ref, out_ref, sem):
    copy = pltpu.make_async_copy(back_ref, out_ref.at[:, back_ref.shape[1] :], sem)
    copy.start()
    copy.wait()


def call(kernel, outs, scratch, us, mib, *args, scalars=0, ins=None, spec=None, aliases=None):
    return pl.pallas_call(
        kernel,
        out_shape=outs,
        in_specs=ins or [SMEM] * scalars + [VMEM] * (len(args) - scalars),
        out_specs=spec or jax.tree.map(lambda _: VMEM, outs),
        scratch_shapes=scratch,
        input_output_aliases=aliases or {},
        cost_estimate=pl.CostEstimate(
            flops=int(us * 1e9), bytes_accessed=1 << 20, transcendentals=0
        ),
        compiler_params=pltpu.CompilerParams(vmem_limit_bytes=min(mib << 20, MOST)),
    )(*args)


def shape(dims, dtype=F32):
    return jax.ShapeDtypeStruct(dims, dtype)


def shifted(x, axis, k):
    n = lax.axis_size(axis)
    return lax.ppermute(x, axis, [(i, (i + k) % n) for i in range(n)])


def mirrored(x, axis):
    n = lax.axis_size(axis)
    return lax.ppermute(x, axis, [(i, n - 1 - i) for i in range(n)])


def body(queries, keys, values, feat_q, feat_k):
    tokens = queries.shape[0]
    heads = feat_q.shape[0]
    side = heads // 2
    depth = lax.axis_size("y")
    at = jnp.stack([lax.axis_index(a) for a in SEQ]).astype(jnp.int32)
    rows = side * tokens
    kv = call(
        pack,
        shape((tokens, F), BF16),
        [pltpu.SemaphoreType.DMA((2,))],
        1,
        1,
        at,
        pltpu.with_memory_space_constraint(keys, pltpu.HBM),
        pltpu.with_memory_space_constraint(values, pltpu.HBM),
        ins=[SMEM] + [HBM] * 2,
    )
    zs = [shifted(kv, "z", k) for k in range(1, lax.axis_size("z"))]
    part = call(halve, shape((tokens, side * D), BF16), [], 0.2, 2, queries)
    part = mirrored(part, "y")
    wk = call(prepare_keys, shape((heads * D, F), BF16), [], 1, 4, feat_k)
    halves = (shape((rows, F), BF16),) * 2
    q2a, qfa = call(functools.partial(prepare, 0), halves, [], 1.5, 4, queries, feat_q)
    zs, wk, q2a, qfa = lax.optimization_barrier((zs, wk, q2a, qfa))
    half = tokens * (1 + len(zs))
    row = call(stack, shape((half, F), BF16), [], 0.1, 2, kv, *zs)
    other = shifted(row, "c", 1)
    partner = mirrored(row, "y")
    next_row = lax.ppermute(row, "y", [(i, i ^ 1) for i in range(depth)])
    far_row = shifted(row, "y", depth // 2)
    many = 2

    def near_part(start, q2, qf, *sources):
        return call(
            functools.partial(own_row, start),
            (shape((rows, F)), shape((rows, D)), shape((rows, F))),
            [pltpu.VMEM((2 * half, F), BF16)] * 2
            + [pltpu.VMEM((tokens, tokens), F32)] * 2
            + [pltpu.VMEM((many * tokens, 2 * half), F32)] * 4
            + [pltpu.VMEM((many * F, 2 * half), BF16)] * 2
            + [pltpu.VMEM((many * tokens, 2 * half), BF16)] * 4,
            6,
            18,
            at,
            q2,
            qf,
            wk,
            *sources,
            scalars=1,
        )

    acca, ma, neara = near_part(0, q2a, qfa, row, other)
    part, partner, acca = lax.optimization_barrier((part, partner, acca))
    partner_other = shifted(partner, "c", 1)
    q2b, qfb = call(functools.partial(prepare, side), halves, [], 1.5, 4, part, feat_q)
    accb, mb, nearb = near_part(side, q2b, qfb, partner, partner_other)
    above = (next_row, far_row)
    above, acca, accb = lax.optimization_barrier((above, acca, accb))
    above_other = []
    for a in above:
        above_other.append(shifted(a, "c", 1))
    above = [partner, *above]
    above_other = [partner_other, *above_other]
    earlier = (depth - 1) * half
    state = call(
        earlier_state,
        shape((heads * F, F), BF16),
        [pltpu.VMEM((earlier, F), BF16)] * 2
        + [pltpu.VMEM((heads * F, F), F32)]
        + [pltpu.VMEM((2 * D, half), F32)] * 2
        + [pltpu.VMEM((2 * F, half), BF16)] * 2,
        6,
        14,
        at,
        wk,
        row,
        *above,
        scalars=1,
    )
    state_other = shifted(state, "c", 1)
    pairs = [r for pair in zip([row, *above], [other, *above_other]) for r in pair]
    acc = call(
        earlier_teacher,
        shape((2 * rows, F)),
        [pltpu.VMEM((2 * earlier, F), BF16)] * 2
        + [pltpu.VMEM((2 * rows, F), BF16), pltpu.VMEM((2 * rows, D), F32)]
        + [pltpu.VMEM((4 * tokens, 2 * half), F32)] * 2
        + [pltpu.VMEM((4 * tokens, 2 * half), BF16)] * 2,
        6,
        18,
        at,
        q2a,
        q2b,
        acca,
        accb,
        ma,
        mb,
        *pairs,
        scalars=1,
    )
    parts = lax.axis_size("x") * lax.axis_size("w")
    grid = (parts, tokens // parts)
    part_shape = shape((tokens, side * D), BF16)
    theirs, loss_b = call(
        functools.partial(finish, side),
        (part_shape, shape(grid)),
        [pltpu.VMEM((tokens, D), F32)],
        1,
        4,
        qfb,
        nearb,
        state,
        state_other,
        acc,
    )
    loss_b = mirrored(loss_b, "y")
    back = mirrored(theirs, "y")
    student, loss = call(
        finish_mine,
        (shape((tokens, heads * D), BF16), shape(grid)),
        [
            pltpu.VMEM((tokens, D), F32),
            pltpu.VMEM((tokens, side * D), BF16),
            pltpu.SemaphoreType.DMA,
        ],
        1,
        4,
        qfa,
        neara,
        state,
        state_other,
        acc,
        spec=(ANY, VMEM),
    )
    loss = loss + loss_b
    tiles = lax.all_to_all(loss[:, None, :], ("x", "w"), 0, 0, tiled=True)
    token_loss = jnp.sum(tiles, axis=(0, 1))
    student = call(
        join,
        shape((tokens, heads * D), BF16),
        [pltpu.SemaphoreType.DMA],
        1,
        2,
        back,
        student,
        ins=[VMEM, ANY],
        spec=ANY,
        aliases={1: 0},
    )
    return student, token_loss


def solution(mesh):
    grid = Mesh(mesh.devices.reshape(4, 4, 2, 4, 2), (*SEQ, "x", "w"))
    head = ("x", "w")
    placed = P(SEQ, head)
    return jax.shard_map(
        body,
        mesh=grid,
        in_specs=(placed, placed, placed, P(head), P(head)),
        out_specs=(placed, P((*SEQ, *head))),
        check_vma=False,
    )
```

```python
import functools
import math

import jax
import jax.numpy as jnp
from jax import lax
from jax.experimental import pallas as pl
from jax.experimental.pallas import tpu as pltpu
from jax.sharding import Mesh
from jax.sharding import PartitionSpec as P


HQ = 128
D = 128
F = 2 * D
LOG2E = math.log2(math.e)
SCALE = LOG2E / math.sqrt(D)
NEG = -1e30
MOST = 67043328
SEQ = ("y", "z", "c")
F32, BF16 = jnp.float32, jnp.bfloat16
VMEM = pl.BlockSpec(memory_space=pltpu.VMEM)
SMEM = pl.BlockSpec(memory_space=pltpu.SMEM)
ANY = pl.BlockSpec(memory_space=pl.ANY)
HBM = pl.BlockSpec(memory_space=pltpu.HBM)


def mm(a, b):
    return jnp.dot(a, b, preferred_element_type=F32)


def mm_t(a, b):
    return lax.dot_general(a, b, (((1,), (1,)), ((), ())), preferred_element_type=F32)


def split(x):
    high = x.astype(BF16)
    return high, (x - high.astype(F32)).astype(BF16)


def both_softmax(x, axis):
    up = jnp.exp2(x - jnp.max(x, axis, keepdims=True))
    down = jnp.exp2(jnp.min(x, axis, keepdims=True) - x)
    up = up * (1.0 / jnp.sum(up, axis, keepdims=True))
    down = down * (1.0 / jnp.sum(down, axis, keepdims=True))
    return up.astype(BF16), down.astype(BF16)


def prepare(start, q_ref, fq_ref, q2_ref, qf_ref):
    tokens = q_ref.shape[0]

    def head(h, _):
        q = q_ref[:, pl.ds(pl.multiple_of(h * D, D), D)]
        rows = pl.ds(pl.multiple_of(h * tokens, tokens), tokens)
        high, low = split(q.astype(F32) * SCALE)
        q2_ref[rows, :D] = high
        q2_ref[rows, D:] = low
        up, down = both_softmax(mm(q, fq_ref[start + h]) * LOG2E, 1)
        qf_ref[rows, :D] = up
        qf_ref[rows, D:] = down
        return 0

    lax.fori_loop(0, q2_ref.shape[0] // tokens, head, 0, unroll=4)


def prepare_keys(fk_ref, wk_ref):
    def head(h, _):
        high, low = split((fk_ref[h].astype(F32) * LOG2E).T)
        rows = pl.ds(pl.multiple_of(h * D, D), D)
        wk_ref[rows, :D] = high
        wk_ref[rows, D:] = low
        return 0

    lax.fori_loop(0, fk_ref.shape[0], head, 0, unroll=4)


def lane_blocks(s):
    return [s[:, i : i + D] for i in range(0, s.shape[1], D)]


def row_max(parts):
    while len(parts) > 1:
        parts = [jnp.maximum(a, b) for a, b in zip(parts[::2], parts[1::2])]
    return jnp.max(parts[0], 1, keepdims=True)


def own_row(start, at_ref, q2_ref, qf_ref, wk_ref, *refs):
    rows, refs = refs[:-17], refs[-17:]
    acc_ref, m_ref, near_ref, k2, v1, bias, keep = refs[:7]
    s0, s1, x0, x1, f0, f1, p0, p1, a0, a1 = refs[7:]
    tokens = keep.shape[0]
    heads = qf_ref.shape[0] // tokens
    half = rows[0].shape[0]
    wide = k2.shape[0]
    many = s0.shape[0] // tokens
    groups = heads // many
    tile = wide // many
    z, c = at_ref[1], at_ref[2]
    safe = jnp.broadcast_to(rows[0][:16, :D].astype(F32)[:1], (tokens, D))
    for side, ref in enumerate(rows):
        for slot in range(half // tokens):
            kv = ref[slot * tokens : (slot + 1) * tokens].astype(F32)
            key, value, one = kv[:, :D], kv[:, D:], jnp.ones((tokens, D), F32)
            if slot or side:
                seen = slot <= z if slot else c == 1
                key = jnp.where(seen, key, safe)
                value = jnp.where(seen, value, 0.0)
                one = jnp.where(seen, one, 0.0)
            here = slice(side * half + slot * tokens, side * half + (slot + 1) * tokens)
            k2[here, :D] = key.astype(BF16)
            k2[here, D:] = key.astype(BF16)
            v1[here, :D] = value.astype(BF16)
            v1[here, D:] = one.astype(BF16)
    row = lax.broadcasted_iota(jnp.int32, (tokens, tokens), 0)
    col = lax.broadcasted_iota(jnp.int32, (tokens, tokens), 1)
    seen = (col <= row).astype(F32)
    keep[...] = seen
    bias[...] = (1.0 - seen) * NEG

    def block(g, size):
        return pl.ds(pl.multiple_of(g * size, size), size)

    def first(g, s, x, j):
        cols = slice(j * tile, (j + 1) * tile)
        s[:, cols] = mm_t(q2_ref[block(g, many * tokens)], k2[cols])
        x[:, cols] = mm_t(wk_ref[block(start // many + g, many * D)], k2[cols])

    def second(g, s, x, p, f, i):
        here = slice(i * tokens, (i + 1) * tokens)
        parts = lane_blocks(s[here])
        parts[0] = parts[0] + bias[...]
        m = row_max(parts)
        m_ref[block(g * many + i, tokens)] = jnp.broadcast_to(m, (tokens, D))
        p[here] = jnp.concatenate([jnp.exp2(a - m).astype(BF16) for a in parts], 1)
        up, down = both_softmax(x[i * D : (i + 1) * D], 0)
        f[i * F : i * F + D] = up
        f[i * F + D : (i + 1) * F] = down

    def third(g, f, a, i):
        here = slice(i * tokens, (i + 1) * tokens)
        scores = mm(qf_ref[block(g * many + i, tokens)], f[i * F : (i + 1) * F])
        a[here, :D] = (scores[:, :D] * keep[...]).astype(BF16)
        a[here, D:] = scores[:, D:].astype(BF16)

    def mix(out_ref, g, p):
        out_ref[block(g, many * tokens)] = mm(p[...], v1[...])

    def stage(g, s, x, p, f, s_next, x_next, p_last, f_last, a_last, a_older):
        last, older = jnp.maximum(g - 1, 0), jnp.maximum(g - 2, 0)
        for j in range(many):
            first(jnp.minimum(g + 1, groups - 1), s_next, x_next, j)
            second(g, s, x, p, f, j)
            third(last, f_last, a_last, j)
            if j == 0:
                mix(acc_ref, last, p_last)
            if j == many // 2:
                mix(near_ref, older, a_older)

    for j in range(many):
        first(0, s0, x0, j)
    f1[...] = jnp.zeros_like(f1)
    p1[...] = jnp.zeros_like(p1)
    a0[...] = jnp.zeros_like(a0)

    def step(i, _):
        g = 2 * i
        stage(g, s0, x0, p0, f0, s1, x1, p1, f1, a1, a0)
        stage(g + 1, s1, x1, p1, f1, s0, x0, p0, f0, a0, a1)
        return 0

    lax.fori_loop(0, groups // 2, step, 0)
    mix(acc_ref, groups - 1, p1)
    mix(near_ref, groups - 2, a0)
    for j in range(many):
        third(groups - 1, f1, a1, j)
    mix(near_ref, groups - 1, a1)


def absolute(at_ref, rows, store):
    depth = len(rows)
    y = at_ref[0]
    places = (y, depth - 1 - y, y + 1 - 2 * lax.rem(y, 2), lax.rem(y + depth // 2, depth))
    for r, refs in zip(places, rows):

        @pl.when(r < depth - 1)
        def _(r=r, refs=refs):
            store(r, refs)


def fill_at(k2, v1, at, size, kv):
    here = pl.ds(pl.multiple_of(at, size), size)
    k2[here, :D] = kv[:, :D]
    k2[here, D:] = kv[:, :D]
    v1[here, :D] = kv[:, D:]
    v1[here, D:] = jnp.ones((size, D), BF16)


def unit_of(at_ref, u, half_heads):
    mine = u < at_ref[0]
    return jnp.where(mine, u, u - at_ref[0]), jnp.where(mine, 0, half_heads)


def earlier_state(at_ref, wk_ref, *refs):
    rows, (out_ref, k2, v1, state, x0, x1, f0, f1) = refs[:-8], refs[-8:]
    heads = out_ref.shape[0] // F
    half = rows[0].shape[0]
    pairs = heads // 4
    count = (len(rows) - 1) * pairs
    state[...] = jnp.zeros_like(state)
    f1[...] = jnp.zeros_like(f1)
    absolute(at_ref, rows, lambda r, ref: fill_at(k2, v1, r * half, half, ref[...]))

    def place(t):
        t = jnp.clip(t, 0, count - 1)
        r, head = unit_of(at_ref, lax.div(t, pairs), heads // 2)
        head = head + 2 * lax.rem(t, pairs)
        return pl.ds(pl.multiple_of(r * half, half), half), head

    def first(t, x):
        at, head = place(t)
        x[...] = mm_t(wk_ref[pl.ds(pl.multiple_of(head * D, 2 * D), 2 * D)], k2[at])

    def second(x, f):
        for i in range(2):
            up, down = both_softmax(x[i * D : (i + 1) * D], 0)
            f[i * F : i * F + D] = up
            f[i * F + D : (i + 1) * F] = down

    def third(t, f):
        at, head = place(t)
        state[pl.ds(pl.multiple_of(head * F, 2 * F), 2 * F)] += mm(f[...], v1[at])

    first(0, x0)

    def step(i, _):
        t = 2 * i
        first(t + 1, x1)
        second(x0, f0)
        third(t - 1, f1)
        first(t + 2, x0)
        second(x1, f1)
        third(t, f0)
        return 0

    lax.fori_loop(0, count // 2, step, 0)
    third(count - 1, f1)
    out_ref[...] = state[...].astype(BF16)


def earlier_teacher(at_ref, q2a_ref, q2b_ref, acca_ref, accb_ref, ma_ref, mb_ref, *refs):
    rows, (acc, k2, v1, q2, m_all, s0, s1, p0, p1) = refs[:-9], refs[-9:]
    half = rows[0].shape[0]
    wide = 2 * half
    part = s0.shape[0]
    side = q2a_ref.shape[0]
    groups = side // part
    pairs = [rows[i : i + 2] for i in range(0, len(rows), 2)]
    count = (len(pairs) - 1) * groups
    for i, (q2_ref, acc_ref, m_ref) in enumerate(
        ((q2a_ref, acca_ref, ma_ref), (q2b_ref, accb_ref, mb_ref))
    ):
        here = slice(i * side, (i + 1) * side)
        q2[here] = q2_ref[...]
        acc[here] = acc_ref[...]
        m_all[here] = m_ref[...]

    def store(r, pair):
        for i, ref in enumerate(pair):
            fill_at(k2, v1, r * wide + i * half, half, ref[...])

    absolute(at_ref, pairs, store)

    def place(t):
        t = jnp.clip(t, 0, count - 1)
        r, at = unit_of(at_ref, lax.div(t, groups), side)
        at = pl.multiple_of(at + lax.rem(t, groups) * part, part)
        return pl.ds(pl.multiple_of(r * wide, wide), wide), at

    def first(t, s):
        at, g = place(t)
        s[...] = mm_t(q2[pl.ds(g, part)], k2[at])

    def second(t, s, p):
        _, g = place(t)
        for i in range(0, part, D):
            here = pl.ds(pl.multiple_of(g + i, D), D)
            before = m_all[here]
            m = jnp.maximum(before, row_max(lane_blocks(s[i : i + D])))
            m_all[here] = m
            factor = jnp.exp2(before - m)
            acc[here] = acc[here] * jnp.concatenate([factor, factor], 1)
            m = jnp.concatenate([m] * (wide // D), 1)
            p[i : i + D] = jnp.exp2(s[i : i + D] - m).astype(BF16)

    def third(t, p):
        at, g = place(t)
        acc[pl.ds(g, part)] += mm(p[...], v1[at])

    first(0, s0)

    def step(i, _):
        t = 2 * i
        first(t + 1, s1)
        second(t, s0, p0)
        third(t, p0)
        first(t + 2, s0)
        second(t + 1, s1, p1)
        third(t + 1, p1)
        return 0

    lax.fori_loop(0, count // 2, step, 0)


def by_place(total, blocks, width):
    tokens = total.shape[0]
    per_token = jnp.sum(total.T, 0, keepdims=True) * (1.0 / HQ)
    t = lax.broadcasted_iota(jnp.int32, (blocks, tokens), 1)
    b = lax.broadcasted_iota(jnp.int32, (blocks, tokens), 0)
    own = (t >= b * width) & (t < (b + 1) * width)
    ti = lax.broadcasted_iota(jnp.int32, (tokens, width), 0)
    ji = lax.broadcasted_iota(jnp.int32, (tokens, width), 1)
    pick = jnp.zeros((tokens, width), F32)
    for i in range(blocks):
        pick = pick + (ti == ji + i * width).astype(F32)
    return jnp.dot(
        jnp.where(own, jnp.broadcast_to(per_token, (blocks, tokens)), 0.0),
        pick,
        precision=lax.Precision.HIGHEST,
        preferred_element_type=F32,
    )


def finish(start, qf_ref, near_ref, mine_ref, other_ref, acc_ref, out_ref, loss_ref, total):
    tokens = total.shape[0]
    total[...] = jnp.zeros_like(total)
    for h in range(qf_ref.shape[0] // tokens):
        here = slice(h * tokens, (h + 1) * tokens)
        there = slice((start + h) * F, (start + h + 1) * F)
        qf = qf_ref[here]
        sums = near_ref[here] + mm(qf, mine_ref[there]) + mm(qf, other_ref[there])
        student = sums[:, :D] * (1.0 / sums[:, D:])
        out_ref[:, h * D : (h + 1) * D] = student.astype(BF16)
        acc = acc_ref[(start + h) * tokens : (start + h + 1) * tokens]
        total[...] += (student - acc[:, :D] * (1.0 / acc[:, D:])) ** 2
    loss_ref[...] = by_place(total[...], *loss_ref.shape)


def finish_mine(qf_ref, near_ref, mine_ref, other_ref, acc_ref, student_ref, loss_ref, total, out, sem):
    finish(0, qf_ref, near_ref, mine_ref, other_ref, acc_ref, out, loss_ref, total)
    copy = pltpu.make_async_copy(out, student_ref.at[:, : out.shape[1]], sem)
    copy.start()
    copy.wait()


def move(pairs, sems):
    copies = [pltpu.make_async_copy(a, b, sems.at[i]) for i, (a, b) in enumerate(pairs)]
    for copy in copies:
        copy.start()
    for copy in copies:
        copy.wait()


def stack(*refs):
    size = refs[0].shape[0]
    for i, ref in enumerate(refs[:-1]):
        refs[-1][i * size : (i + 1) * size] = ref[...]


def pack(at_ref, place_ref, keys_ref, values_ref, kv_ref, sems):
    move(((keys_ref, kv_ref.at[:, :D]), (values_ref, kv_ref.at[:, D:])), sems)


def halve(q_ref, part_ref):
    part_ref[...] = q_ref[:, part_ref.shape[1] :]


def join(back_ref, student_ref, out_ref, sem):
    copy = pltpu.make_async_copy(back_ref, out_ref.at[:, back_ref.shape[1] :], sem)
    copy.start()
    copy.wait()


def to_x(at_ref, a_ref, b_ref, *refs):
    held = refs[-1]
    held[...] = a_ref[...] + b_ref[...]
    n = len(refs) - 1
    rows = held.shape[0] // n
    for k in range(n):
        refs[k][...] = held[pl.ds(lax.rem(at_ref[0] + k, n) * rows, rows)]


def to_w(at_ref, *refs):
    parts, (keep_ref, send_ref, held) = refs[:-3], refs[-3:]
    total = parts[0][...]
    for ref in parts[1:]:
        total = total + ref[...]
    held[...] = total
    keep_ref[...] = held[pl.ds(at_ref[1], 1)]
    send_ref[...] = held[pl.ds(1 - at_ref[1], 1)]


def add(a_ref, b_ref, out_ref):
    out_ref[...] = a_ref[...] + b_ref[...]


def call(kernel, outs, scratch, us, mib, *args, scalars=0, ins=None, spec=None, aliases=None):
    return pl.pallas_call(
        kernel,
        out_shape=outs,
        in_specs=ins or [SMEM] * scalars + [VMEM] * (len(args) - scalars),
        out_specs=spec or jax.tree.map(lambda _: VMEM, outs),
        scratch_shapes=scratch,
        input_output_aliases=aliases or {},
        cost_estimate=pl.CostEstimate(
            flops=int(us * 1e9), bytes_accessed=1 << 20, transcendentals=0
        ),
        compiler_params=pltpu.CompilerParams(vmem_limit_bytes=min(mib << 20, MOST)),
    )(*args)


def shape(dims, dtype=F32):
    return jax.ShapeDtypeStruct(dims, dtype)


def shifted(x, axis, k):
    n = lax.axis_size(axis)
    return lax.ppermute(x, axis, [(i, (i + k) % n) for i in range(n)])


def mirrored(x, axis):
    n = lax.axis_size(axis)
    return lax.ppermute(x, axis, [(i, n - 1 - i) for i in range(n)])


def body(queries, keys, values, feat_q, feat_k):
    tokens = queries.shape[0]
    heads = feat_q.shape[0]
    side = heads // 2
    depth = lax.axis_size("y")
    at = jnp.stack([lax.axis_index(a) for a in SEQ]).astype(jnp.int32)
    place = jnp.stack([lax.axis_index(a) for a in ("x", "w")]).astype(jnp.int32)
    rows = side * tokens
    kv = call(
        pack,
        shape((tokens, F), BF16),
        [pltpu.SemaphoreType.DMA((2,))],
        1,
        1,
        at,
        place,
        pltpu.with_memory_space_constraint(keys, pltpu.HBM),
        pltpu.with_memory_space_constraint(values, pltpu.HBM),
        ins=[SMEM] * 2 + [HBM] * 2,
    )
    zs = [shifted(kv, "z", k) for k in range(1, lax.axis_size("z"))]
    part = call(halve, shape((tokens, side * D), BF16), [], 0.2, 2, queries)
    part = mirrored(part, "y")
    wk = call(prepare_keys, shape((heads * D, F), BF16), [], 1, 4, feat_k)
    halves = (shape((rows, F), BF16),) * 2
    q2a, qfa = call(functools.partial(prepare, 0), halves, [], 1.5, 4, queries, feat_q)
    zs, wk, q2a, qfa = lax.optimization_barrier((zs, wk, q2a, qfa))
    half = tokens * (1 + len(zs))
    row = call(stack, shape((half, F), BF16), [], 0.1, 2, kv, *zs)
    other = shifted(row, "c", 1)
    partner = mirrored(row, "y")
    next_row = lax.ppermute(row, "y", [(i, i ^ 1) for i in range(depth)])
    far_row = shifted(row, "y", depth // 2)
    many = 2

    def near_part(start, q2, qf, *sources):
        return call(
            functools.partial(own_row, start),
            (shape((rows, F)), shape((rows, D)), shape((rows, F))),
            [pltpu.VMEM((2 * half, F), BF16)] * 2
            + [pltpu.VMEM((tokens, tokens), F32)] * 2
            + [pltpu.VMEM((many * tokens, 2 * half), F32)] * 4
            + [pltpu.VMEM((many * F, 2 * half), BF16)] * 2
            + [pltpu.VMEM((many * tokens, 2 * half), BF16)] * 4,
            6,
            18,
            at,
            q2,
            qf,
            wk,
            *sources,
            scalars=1,
        )

    acca, ma, neara = near_part(0, q2a, qfa, row, other)
    part, partner, acca = lax.optimization_barrier((part, partner, acca))
    partner_other = shifted(partner, "c", 1)
    q2b, qfb = call(functools.partial(prepare, side), halves, [], 1.5, 4, part, feat_q)
    accb, mb, nearb = near_part(side, q2b, qfb, partner, partner_other)
    above = (next_row, far_row)
    above, acca, accb = lax.optimization_barrier((above, acca, accb))
    above_other = []
    for a in above:
        above_other.append(shifted(a, "c", 1))
    above = [partner, *above]
    above_other = [partner_other, *above_other]
    earlier = (depth - 1) * half
    state = call(
        earlier_state,
        shape((heads * F, F), BF16),
        [pltpu.VMEM((earlier, F), BF16)] * 2
        + [pltpu.VMEM((heads * F, F), F32)]
        + [pltpu.VMEM((2 * D, half), F32)] * 2
        + [pltpu.VMEM((2 * F, half), BF16)] * 2,
        6,
        14,
        at,
        wk,
        row,
        *above,
        scalars=1,
    )
    state_other = shifted(state, "c", 1)
    pairs = [r for pair in zip([row, *above], [other, *above_other]) for r in pair]
    acc = call(
        earlier_teacher,
        shape((2 * rows, F)),
        [pltpu.VMEM((2 * earlier, F), BF16)] * 2
        + [pltpu.VMEM((2 * rows, F), BF16), pltpu.VMEM((2 * rows, D), F32)]
        + [pltpu.VMEM((4 * tokens, 2 * half), F32)] * 2
        + [pltpu.VMEM((4 * tokens, 2 * half), BF16)] * 2,
        6,
        18,
        at,
        q2a,
        q2b,
        acca,
        accb,
        ma,
        mb,
        *pairs,
        scalars=1,
    )
    parts = lax.axis_size("x") * lax.axis_size("w")
    grid = (parts, tokens // parts)
    part_shape = shape((tokens, side * D), BF16)
    theirs, loss_b = call(
        functools.partial(finish, side),
        (part_shape, shape(grid)),
        [pltpu.VMEM((tokens, D), F32)],
        1,
        4,
        qfb,
        nearb,
        state,
        state_other,
        acc,
    )
    loss_b = mirrored(loss_b, "y")
    back = mirrored(theirs, "y")
    student, loss = call(
        finish_mine,
        (shape((tokens, heads * D), BF16), shape(grid)),
        [
            pltpu.VMEM((tokens, D), F32),
            pltpu.VMEM((tokens, side * D), BF16),
            pltpu.SemaphoreType.DMA,
        ],
        1,
        4,
        qfa,
        neara,
        state,
        state_other,
        acc,
        spec=(ANY, VMEM),
    )
    width = tokens // parts
    nx, nw = lax.axis_size("x"), lax.axis_size("w")
    pieces = call(
        to_x,
        (shape((nw, width)),) * nx,
        [pltpu.VMEM(grid, F32)],
        0.1,
        1,
        place,
        loss,
        loss_b,
        scalars=1,
    )
    parts_x = [pieces[0]]
    for k in range(1, nx):
        parts_x.append(shifted(pieces[k], "x", k))
    keep, send = call(
        to_w,
        (shape((1, width)),) * 2,
        [pltpu.VMEM((nw, width), F32)],
        0.1,
        1,
        place,
        *parts_x,
        scalars=1,
    )
    got = mirrored(send, "w")
    token_loss = call(add, shape((1, width)), [], 0.1, 1, keep, got).reshape(width)
    student = call(
        join,
        shape((tokens, heads * D), BF16),
        [pltpu.SemaphoreType.DMA],
        1,
        2,
        back,
        student,
        ins=[VMEM, ANY],
        spec=ANY,
        aliases={1: 0},
    )
    return student, token_loss


def solution(mesh):
    grid = Mesh(mesh.devices.reshape(4, 4, 2, 4, 2), (*SEQ, "x", "w"))
    head = ("x", "w")
    placed = P(SEQ, head)
    return jax.shard_map(
        body,
        mesh=grid,
        in_specs=(placed, placed, placed, P(head), P(head)),
        out_specs=(placed, P((*SEQ, *head))),
        check_vma=False,
    )
```

```python
import functools
import math

import jax
import jax.numpy as jnp
from jax import lax
from jax.experimental import pallas as pl
from jax.experimental.pallas import tpu as pltpu
from jax.sharding import Mesh
from jax.sharding import PartitionSpec as P


HQ = 128
D = 128
F = 2 * D
LOG2E = math.log2(math.e)
SCALE = LOG2E / math.sqrt(D)
NEG = -1e30
MOST = 67043328
SEQ = ("y", "z", "c")
F32, BF16 = jnp.float32, jnp.bfloat16
VMEM = pl.BlockSpec(memory_space=pltpu.VMEM)
SMEM = pl.BlockSpec(memory_space=pltpu.SMEM)
ANY = pl.BlockSpec(memory_space=pl.ANY)
HBM = pl.BlockSpec(memory_space=pltpu.HBM)


def place_of(at_ref, name):
    sizes = {"w": 2, "x": 4, "c": 2, "z": 4, "y": 4}
    below = 1
    for axis, size in sizes.items():
        if axis == name:
            return lax.rem(lax.div(at_ref[0], below), size)
        below *= size


def mm(a, b):
    return jnp.dot(a, b, preferred_element_type=F32)


def mm_t(a, b):
    return lax.dot_general(a, b, (((1,), (1,)), ((), ())), preferred_element_type=F32)


def split(x):
    high = x.astype(BF16)
    return high, (x - high.astype(F32)).astype(BF16)


def both_softmax(x, axis):
    up = jnp.exp2(x - jnp.max(x, axis, keepdims=True))
    down = jnp.exp2(jnp.min(x, axis, keepdims=True) - x)
    up = up * (1.0 / jnp.sum(up, axis, keepdims=True))
    down = down * (1.0 / jnp.sum(down, axis, keepdims=True))
    return up.astype(BF16), down.astype(BF16)


def prepare(start, q_ref, fq_ref, q2_ref, qf_ref):
    tokens = q_ref.shape[0]

    def head(h, _):
        q = q_ref[:, pl.ds(pl.multiple_of(h * D, D), D)]
        rows = pl.ds(pl.multiple_of(h * tokens, tokens), tokens)
        high, low = split(q.astype(F32) * SCALE)
        q2_ref[rows, :D] = high
        q2_ref[rows, D:] = low
        up, down = both_softmax(mm(q, fq_ref[start + h]) * LOG2E, 1)
        qf_ref[rows, :D] = up
        qf_ref[rows, D:] = down
        return 0

    lax.fori_loop(0, q2_ref.shape[0] // tokens, head, 0, unroll=4)


def prepare_keys(fk_ref, wk_ref):
    def head(h, _):
        high, low = split((fk_ref[h].astype(F32) * LOG2E).T)
        rows = pl.ds(pl.multiple_of(h * D, D), D)
        wk_ref[rows, :D] = high
        wk_ref[rows, D:] = low
        return 0

    lax.fori_loop(0, fk_ref.shape[0], head, 0, unroll=4)


def lane_blocks(s):
    return [s[:, i : i + D] for i in range(0, s.shape[1], D)]


def row_max(parts):
    while len(parts) > 1:
        parts = [jnp.maximum(a, b) for a, b in zip(parts[::2], parts[1::2])]
    return jnp.max(parts[0], 1, keepdims=True)


def own_row(start, at_ref, q2_ref, qf_ref, wk_ref, *refs):
    rows, refs = refs[:-17], refs[-17:]
    acc_ref, m_ref, near_ref, k2, v1, bias, keep = refs[:7]
    s0, s1, x0, x1, f0, f1, p0, p1, a0, a1 = refs[7:]
    tokens = keep.shape[0]
    heads = qf_ref.shape[0] // tokens
    half = rows[0].shape[0]
    wide = k2.shape[0]
    many = s0.shape[0] // tokens
    groups = heads // many
    tile = wide // many
    z, c = place_of(at_ref, "z"), place_of(at_ref, "c")
    safe = jnp.broadcast_to(rows[0][:16, :D].astype(F32)[:1], (tokens, D))
    for side, ref in enumerate(rows):
        for slot in range(half // tokens):
            kv = ref[slot * tokens : (slot + 1) * tokens].astype(F32)
            key, value, one = kv[:, :D], kv[:, D:], jnp.ones((tokens, D), F32)
            if slot or side:
                seen = slot <= z if slot else c == 1
                key = jnp.where(seen, key, safe)
                value = jnp.where(seen, value, 0.0)
                one = jnp.where(seen, one, 0.0)
            here = slice(side * half + slot * tokens, side * half + (slot + 1) * tokens)
            k2[here, :D] = key.astype(BF16)
            k2[here, D:] = key.astype(BF16)
            v1[here, :D] = value.astype(BF16)
            v1[here, D:] = one.astype(BF16)
    row = lax.broadcasted_iota(jnp.int32, (tokens, tokens), 0)
    col = lax.broadcasted_iota(jnp.int32, (tokens, tokens), 1)
    seen = (col <= row).astype(F32)
    keep[...] = seen
    bias[...] = (1.0 - seen) * NEG

    def block(g, size):
        return pl.ds(pl.multiple_of(g * size, size), size)

    def first(g, s, x, j):
        cols = slice(j * tile, (j + 1) * tile)
        s[:, cols] = mm_t(q2_ref[block(g, many * tokens)], k2[cols])
        x[:, cols] = mm_t(wk_ref[block(start // many + g, many * D)], k2[cols])

    def second(g, s, x, p, f, i):
        here = slice(i * tokens, (i + 1) * tokens)
        parts = lane_blocks(s[here])
        parts[0] = parts[0] + bias[...]
        m = row_max(parts)
        m_ref[block(g * many + i, tokens)] = jnp.broadcast_to(m, (tokens, D))
        p[here] = jnp.concatenate([jnp.exp2(a - m).astype(BF16) for a in parts], 1)
        up, down = both_softmax(x[i * D : (i + 1) * D], 0)
        f[i * F : i * F + D] = up
        f[i * F + D : (i + 1) * F] = down

    def third(g, f, a, i):
        here = slice(i * tokens, (i + 1) * tokens)
        scores = mm(qf_ref[block(g * many + i, tokens)], f[i * F : (i + 1) * F])
        a[here, :D] = (scores[:, :D] * keep[...]).astype(BF16)
        a[here, D:] = scores[:, D:].astype(BF16)

    def mix(out_ref, g, p):
        out_ref[block(g, many * tokens)] = mm(p[...], v1[...])

    def stage(g, s, x, p, f, s_next, x_next, p_last, f_last, a_last, a_older):
        last, older = jnp.maximum(g - 1, 0), jnp.maximum(g - 2, 0)
        for j in range(many):
            first(jnp.minimum(g + 1, groups - 1), s_next, x_next, j)
            second(g, s, x, p, f, j)
            third(last, f_last, a_last, j)
            if j == 0:
                mix(acc_ref, last, p_last)
            if j == many // 2:
                mix(near_ref, older, a_older)

    for j in range(many):
        first(0, s0, x0, j)
    f1[...] = jnp.zeros_like(f1)
    p1[...] = jnp.zeros_like(p1)
    a0[...] = jnp.zeros_like(a0)

    def step(i, _):
        g = 2 * i
        stage(g, s0, x0, p0, f0, s1, x1, p1, f1, a1, a0)
        stage(g + 1, s1, x1, p1, f1, s0, x0, p0, f0, a0, a1)
        return 0

    lax.fori_loop(0, groups // 2, step, 0)
    mix(acc_ref, groups - 1, p1)
    mix(near_ref, groups - 2, a0)
    for j in range(many):
        third(groups - 1, f1, a1, j)
    mix(near_ref, groups - 1, a1)


def absolute(at_ref, rows, store):
    depth = len(rows)
    y = place_of(at_ref, "y")
    places = (y, depth - 1 - y, y + 1 - 2 * lax.rem(y, 2), lax.rem(y + depth // 2, depth))
    for r, refs in zip(places, rows):

        @pl.when(r < depth - 1)
        def _(r=r, refs=refs):
            store(r, refs)


def fill_at(k2, v1, at, size, kv):
    here = pl.ds(pl.multiple_of(at, size), size)
    k2[here, :D] = kv[:, :D]
    k2[here, D:] = kv[:, :D]
    v1[here, :D] = kv[:, D:]
    v1[here, D:] = jnp.ones((size, D), BF16)


def unit_of(at_ref, u, half_heads):
    y = place_of(at_ref, "y")
    mine = u < y
    return jnp.where(mine, u, u - y), jnp.where(mine, 0, half_heads)


def earlier_state(at_ref, wk_ref, *refs):
    rows, (out_ref, k2, v1, state, x0, x1, f0, f1) = refs[:-8], refs[-8:]
    heads = out_ref.shape[0] // F
    half = rows[0].shape[0]
    pairs = heads // 4
    count = (len(rows) - 1) * pairs
    state[...] = jnp.zeros_like(state)
    f1[...] = jnp.zeros_like(f1)
    absolute(at_ref, rows, lambda r, ref: fill_at(k2, v1, r * half, half, ref[...]))

    def place(t):
        t = jnp.clip(t, 0, count - 1)
        r, head = unit_of(at_ref, lax.div(t, pairs), heads // 2)
        head = head + 2 * lax.rem(t, pairs)
        return pl.ds(pl.multiple_of(r * half, half), half), head

    def first(t, x):
        at, head = place(t)
        x[...] = mm_t(wk_ref[pl.ds(pl.multiple_of(head * D, 2 * D), 2 * D)], k2[at])

    def second(x, f):
        for i in range(2):
            up, down = both_softmax(x[i * D : (i + 1) * D], 0)
            f[i * F : i * F + D] = up
            f[i * F + D : (i + 1) * F] = down

    def third(t, f):
        at, head = place(t)
        state[pl.ds(pl.multiple_of(head * F, 2 * F), 2 * F)] += mm(f[...], v1[at])

    first(0, x0)

    def step(i, _):
        t = 2 * i
        first(t + 1, x1)
        second(x0, f0)
        third(t - 1, f1)
        first(t + 2, x0)
        second(x1, f1)
        third(t, f0)
        return 0

    lax.fori_loop(0, count // 2, step, 0)
    third(count - 1, f1)
    out_ref[...] = state[...].astype(BF16)


def earlier_teacher(at_ref, q2a_ref, q2b_ref, acca_ref, accb_ref, ma_ref, mb_ref, *refs):
    rows, (acc, k2, v1, q2, m_all, s0, s1, p0, p1) = refs[:-9], refs[-9:]
    half = rows[0].shape[0]
    wide = 2 * half
    part = s0.shape[0]
    side = q2a_ref.shape[0]
    groups = side // part
    pairs = [rows[i : i + 2] for i in range(0, len(rows), 2)]
    count = (len(pairs) - 1) * groups
    for i, (q2_ref, acc_ref, m_ref) in enumerate(
        ((q2a_ref, acca_ref, ma_ref), (q2b_ref, accb_ref, mb_ref))
    ):
        here = slice(i * side, (i + 1) * side)
        q2[here] = q2_ref[...]
        acc[here] = acc_ref[...]
        m_all[here] = m_ref[...]

    def store(r, pair):
        for i, ref in enumerate(pair):
            fill_at(k2, v1, r * wide + i * half, half, ref[...])

    absolute(at_ref, pairs, store)

    def place(t):
        t = jnp.clip(t, 0, count - 1)
        r, at = unit_of(at_ref, lax.div(t, groups), side)
        at = pl.multiple_of(at + lax.rem(t, groups) * part, part)
        return pl.ds(pl.multiple_of(r * wide, wide), wide), at

    def first(t, s):
        at, g = place(t)
        s[...] = mm_t(q2[pl.ds(g, part)], k2[at])

    def second(t, s, p):
        _, g = place(t)
        for i in range(0, part, D):
            here = pl.ds(pl.multiple_of(g + i, D), D)
            before = m_all[here]
            m = jnp.maximum(before, row_max(lane_blocks(s[i : i + D])))
            m_all[here] = m
            factor = jnp.exp2(before - m)
            acc[here] = acc[here] * jnp.concatenate([factor, factor], 1)
            m = jnp.concatenate([m] * (wide // D), 1)
            p[i : i + D] = jnp.exp2(s[i : i + D] - m).astype(BF16)

    def third(t, p):
        at, g = place(t)
        acc[pl.ds(g, part)] += mm(p[...], v1[at])

    first(0, s0)

    def step(i, _):
        t = 2 * i
        first(t + 1, s1)
        second(t, s0, p0)
        third(t, p0)
        first(t + 2, s0)
        second(t + 1, s1, p1)
        third(t + 1, p1)
        return 0

    lax.fori_loop(0, count // 2, step, 0)


def by_place(total, blocks, width):
    tokens = total.shape[0]
    per_token = jnp.sum(total.T, 0, keepdims=True) * (1.0 / HQ)
    t = lax.broadcasted_iota(jnp.int32, (blocks, tokens), 1)
    b = lax.broadcasted_iota(jnp.int32, (blocks, tokens), 0)
    own = (t >= b * width) & (t < (b + 1) * width)
    ti = lax.broadcasted_iota(jnp.int32, (tokens, width), 0)
    ji = lax.broadcasted_iota(jnp.int32, (tokens, width), 1)
    pick = jnp.zeros((tokens, width), F32)
    for i in range(blocks):
        pick = pick + (ti == ji + i * width).astype(F32)
    return jnp.dot(
        jnp.where(own, jnp.broadcast_to(per_token, (blocks, tokens)), 0.0),
        pick,
        precision=lax.Precision.HIGHEST,
        preferred_element_type=F32,
    )


def finish(start, qf_ref, near_ref, mine_ref, other_ref, acc_ref, out_ref, loss_ref, total):
    tokens = total.shape[0]
    total[...] = jnp.zeros_like(total)
    for h in range(qf_ref.shape[0] // tokens):
        here = slice(h * tokens, (h + 1) * tokens)
        there = slice((start + h) * F, (start + h + 1) * F)
        qf = qf_ref[here]
        sums = near_ref[here] + mm(qf, mine_ref[there]) + mm(qf, other_ref[there])
        student = sums[:, :D] * (1.0 / sums[:, D:])
        out_ref[:, h * D : (h + 1) * D] = student.astype(BF16)
        acc = acc_ref[(start + h) * tokens : (start + h + 1) * tokens]
        total[...] += (student - acc[:, :D] * (1.0 / acc[:, D:])) ** 2
    loss_ref[...] = by_place(total[...], *loss_ref.shape)


def finish_mine(qf_ref, near_ref, mine_ref, other_ref, acc_ref, student_ref, loss_ref, total, out, sem):
    finish(0, qf_ref, near_ref, mine_ref, other_ref, acc_ref, out, loss_ref, total)
    copy = pltpu.make_async_copy(out, student_ref.at[:, : out.shape[1]], sem)
    copy.start()
    copy.wait()


def move(pairs, sems):
    copies = [pltpu.make_async_copy(a, b, sems.at[i]) for i, (a, b) in enumerate(pairs)]
    for copy in copies:
        copy.start()
    for copy in copies:
        copy.wait()


def stack(*refs):
    size = refs[0].shape[0]
    for i, ref in enumerate(refs[:-1]):
        refs[-1][i * size : (i + 1) * size] = ref[...]


def pack(at_ref, keys_ref, values_ref, kv_ref, sems):
    move(((keys_ref, kv_ref.at[:, :D]), (values_ref, kv_ref.at[:, D:])), sems)


def halve(q_ref, part_ref):
    part_ref[...] = q_ref[:, part_ref.shape[1] :]


def join(back_ref, student_ref, out_ref, sem):
    copy = pltpu.make_async_copy(back_ref, out_ref.at[:, back_ref.shape[1] :], sem)
    copy.start()
    copy.wait()


def to_x(at_ref, a_ref, b_ref, *refs):
    held = refs[-1]
    held[...] = a_ref[...] + b_ref[...]
    n = len(refs) - 1
    rows = held.shape[0] // n
    for k in range(n):
        refs[k][...] = held[pl.ds(lax.rem(place_of(at_ref, "x") + k, n) * rows, rows)]


def to_w(at_ref, *refs):
    parts, (keep_ref, send_ref, held) = refs[:-3], refs[-3:]
    total = parts[0][...]
    for ref in parts[1:]:
        total = total + ref[...]
    held[...] = total
    w = place_of(at_ref, "w")
    keep_ref[...] = held[pl.ds(w, 1)]
    send_ref[...] = held[pl.ds(1 - w, 1)]


def add(a_ref, b_ref, out_ref):
    out_ref[...] = a_ref[...] + b_ref[...]


def call(kernel, outs, scratch, us, mib, *args, scalars=0, ins=None, spec=None, aliases=None):
    return pl.pallas_call(
        kernel,
        out_shape=outs,
        in_specs=ins or [SMEM] * scalars + [VMEM] * (len(args) - scalars),
        out_specs=spec or jax.tree.map(lambda _: VMEM, outs),
        scratch_shapes=scratch,
        input_output_aliases=aliases or {},
        cost_estimate=pl.CostEstimate(
            flops=int(us * 1e9), bytes_accessed=1 << 20, transcendentals=0
        ),
        compiler_params=pltpu.CompilerParams(vmem_limit_bytes=min(mib << 20, MOST)),
    )(*args)


def shape(dims, dtype=F32):
    return jax.ShapeDtypeStruct(dims, dtype)


def shifted(x, axis, k):
    n = lax.axis_size(axis)
    return lax.ppermute(x, axis, [(i, (i + k) % n) for i in range(n)])


def mirrored(x, axis):
    n = lax.axis_size(axis)
    return lax.ppermute(x, axis, [(i, n - 1 - i) for i in range(n)])


def body(queries, keys, values, feat_q, feat_k):
    tokens = queries.shape[0]
    heads = feat_q.shape[0]
    side = heads // 2
    depth = lax.axis_size("y")
    at = lax.axis_index((*SEQ, "x", "w")).astype(jnp.int32).reshape(1)
    rows = side * tokens
    kv = call(
        pack,
        shape((tokens, F), BF16),
        [pltpu.SemaphoreType.DMA((2,))],
        1,
        1,
        at,
        pltpu.with_memory_space_constraint(keys, pltpu.HBM),
        pltpu.with_memory_space_constraint(values, pltpu.HBM),
        ins=[SMEM] + [HBM] * 2,
    )
    zs = [shifted(kv, "z", k) for k in range(1, lax.axis_size("z"))]
    part = call(halve, shape((tokens, side * D), BF16), [], 0.2, 2, queries)
    part = mirrored(part, "y")
    wk = call(prepare_keys, shape((heads * D, F), BF16), [], 1, 4, feat_k)
    halves = (shape((rows, F), BF16),) * 2
    q2a, qfa = call(functools.partial(prepare, 0), halves, [], 1.5, 4, queries, feat_q)
    zs, wk, q2a, qfa = lax.optimization_barrier((zs, wk, q2a, qfa))
    half = tokens * (1 + len(zs))
    row = call(stack, shape((half, F), BF16), [], 0.1, 2, kv, *zs)
    other = shifted(row, "c", 1)
    partner = mirrored(row, "y")
    next_row = lax.ppermute(row, "y", [(i, i ^ 1) for i in range(depth)])
    far_row = shifted(row, "y", depth // 2)
    many = 2

    def near_part(start, q2, qf, *sources):
        return call(
            functools.partial(own_row, start),
            (shape((rows, F)), shape((rows, D)), shape((rows, F))),
            [pltpu.VMEM((2 * half, F), BF16)] * 2
            + [pltpu.VMEM((tokens, tokens), F32)] * 2
            + [pltpu.VMEM((many * tokens, 2 * half), F32)] * 4
            + [pltpu.VMEM((many * F, 2 * half), BF16)] * 2
            + [pltpu.VMEM((many * tokens, 2 * half), BF16)] * 4,
            6,
            18,
            at,
            q2,
            qf,
            wk,
            *sources,
            scalars=1,
        )

    acca, ma, neara = near_part(0, q2a, qfa, row, other)
    part, partner, acca = lax.optimization_barrier((part, partner, acca))
    partner_other = shifted(partner, "c", 1)
    q2b, qfb = call(functools.partial(prepare, side), halves, [], 1.5, 4, part, feat_q)
    accb, mb, nearb = near_part(side, q2b, qfb, partner, partner_other)
    above = (next_row, far_row)
    above, acca, accb = lax.optimization_barrier((above, acca, accb))
    above_other = []
    for a in above:
        above_other.append(shifted(a, "c", 1))
    above = [partner, *above]
    above_other = [partner_other, *above_other]
    earlier = (depth - 1) * half
    state = call(
        earlier_state,
        shape((heads * F, F), BF16),
        [pltpu.VMEM((earlier, F), BF16)] * 2
        + [pltpu.VMEM((heads * F, F), F32)]
        + [pltpu.VMEM((2 * D, half), F32)] * 2
        + [pltpu.VMEM((2 * F, half), BF16)] * 2,
        6,
        14,
        at,
        wk,
        row,
        *above,
        scalars=1,
    )
    state_other = shifted(state, "c", 1)
    pairs = [r for pair in zip([row, *above], [other, *above_other]) for r in pair]
    acc = call(
        earlier_teacher,
        shape((2 * rows, F)),
        [pltpu.VMEM((2 * earlier, F), BF16)] * 2
        + [pltpu.VMEM((2 * rows, F), BF16), pltpu.VMEM((2 * rows, D), F32)]
        + [pltpu.VMEM((4 * tokens, 2 * half), F32)] * 2
        + [pltpu.VMEM((4 * tokens, 2 * half), BF16)] * 2,
        6,
        18,
        at,
        q2a,
        q2b,
        acca,
        accb,
        ma,
        mb,
        *pairs,
        scalars=1,
    )
    parts = lax.axis_size("x") * lax.axis_size("w")
    grid = (parts, tokens // parts)
    part_shape = shape((tokens, side * D), BF16)
    theirs, loss_b = call(
        functools.partial(finish, side),
        (part_shape, shape(grid)),
        [pltpu.VMEM((tokens, D), F32)],
        1,
        4,
        qfb,
        nearb,
        state,
        state_other,
        acc,
    )
    loss_b = mirrored(loss_b, "y")
    back = mirrored(theirs, "y")
    student, loss = call(
        finish_mine,
        (shape((tokens, heads * D), BF16), shape(grid)),
        [
            pltpu.VMEM((tokens, D), F32),
            pltpu.VMEM((tokens, side * D), BF16),
            pltpu.SemaphoreType.DMA,
        ],
        1,
        4,
        qfa,
        neara,
        state,
        state_other,
        acc,
        spec=(ANY, VMEM),
    )
    width = tokens // parts
    nx, nw = lax.axis_size("x"), lax.axis_size("w")
    pieces = call(
        to_x,
        (shape((nw, width)),) * nx,
        [pltpu.VMEM(grid, F32)],
        0.1,
        1,
        at,
        loss,
        loss_b,
        scalars=1,
    )
    parts_x = [pieces[0]]
    for k in range(1, nx):
        parts_x.append(shifted(pieces[k], "x", k))
    keep, send = call(
        to_w,
        (shape((1, width)),) * 2,
        [pltpu.VMEM((nw, width), F32)],
        0.1,
        1,
        at,
        *parts_x,
        scalars=1,
    )
    got = mirrored(send, "w")
    token_loss = call(add, shape((1, width)), [], 0.1, 1, keep, got).reshape(width)
    student = call(
        join,
        shape((tokens, heads * D), BF16),
        [pltpu.SemaphoreType.DMA],
        1,
        2,
        back,
        student,
        ins=[VMEM, ANY],
        spec=ANY,
        aliases={1: 0},
    )
    return student, token_loss


def solution(mesh):
    grid = Mesh(mesh.devices.reshape(4, 4, 2, 4, 2), (*SEQ, "x", "w"))
    head = ("x", "w")
    placed = P(SEQ, head)
    return jax.shard_map(
        body,
        mesh=grid,
        in_specs=(placed, placed, placed, P(head), P(head)),
        out_specs=(placed, P((*SEQ, *head))),
        check_vma=False,
    )
```
